32 devices in a mesh: dp: 8 (over z, x), sp: 4 (over y, core).
Axes of the slice: x: 2, y: 2, z: 4, core: 2. Of those that a mesh axis runs over, the one named last changes fastest.
Arguments:
- inputs: bfloat16 [16, 512, 768], P('dp', 'sp'), may hold values from -6 to 6
- cotangent: bfloat16 [16, 512, 768], P('dp', 'sp'), may hold values from -6 to 6
- joined_weight: bfloat16 [768, 2304], P(('dp', 'sp')), may hold values from -0.21875 to 0.21875
- joined_bias: bfloat16 [2304], P(('dp', 'sp')), may hold values from -3 to 3
- dense_weight: bfloat16 [768, 768], P(('dp', 'sp')), may hold values from -1.75 to 1.75
- dense_bias: bfloat16 [768], P(('dp', 'sp')), may hold values from -3 to 3
- expand_weight: bfloat16 [768, 3072], P(('dp', 'sp')), may hold values from -0.21875 to 0.21875
- expand_bias: bfloat16 [3072], P(('dp', 'sp')), may hold values from -3 to 3
- shrink_weight: bfloat16 [3072, 768], P(('dp', 'sp')), may hold values from -0.109375 to 0.109375
- shrink_bias: bfloat16 [768], P(('dp', 'sp')), may hold values from -3 to 3
- attn_gain: bfloat16 [768], P(('dp', 'sp')), may hold values from 0.5 to 1.5
- attn_shift: bfloat16 [768], P(('dp', 'sp')), may hold values from -3 to 3
- mlp_gain: bfloat16 [768], P(('dp', 'sp')), may hold values from 0.5 to 1.5
- mlp_shift: bfloat16 [768], P(('dp', 'sp')), may hold values from -3 to 3
Outputs:
- output: bfloat16 [16, 512, 768], P('dp', 'sp')
- input_grad: float32 [16, 512, 768], P('dp', 'sp')
- joined_weight_grad: float32 [768, 2304], P(('dp', 'sp'))
- joined_bias_grad: float32 [2304], P(('dp', 'sp'))
- dense_weight_grad: float32 [768, 768], P(('dp', 'sp'))
- dense_bias_grad: float32 [768], P(('dp', 'sp'))
- expand_weight_grad: float32 [768, 3072], P(('dp', 'sp'))
- expand_bias_grad: float32 [3072], P(('dp', 'sp'))
- shrink_weight_grad: float32 [3072, 768], P(('dp', 'sp'))
- shrink_bias_grad: float32 [768], P(('dp', 'sp'))
- attn_gain_grad: float32 [768], P(('dp', 'sp'))
- attn_shift_grad: float32 [768], P(('dp', 'sp'))
- mlp_gain_grad: float32 [768], P(('dp', 'sp'))
- mlp_shift_grad: float32 [768], P(('dp', 'sp'))
The draws below stay inside these ranges and needn't reach their ends.
All inputs are finite; a program needn't handle non-finite values.
Results may differ from the reference program's by a relative error of at most 0.011.
Values may be sent and summed in bfloat16 or wider, within the bound.
No kernel may reach another device: no remote copies, remote signals or barrier semaphores. Data moves between devices by JAX's collectives and lax.ppermute only.
A program may use at most 128 MiB of HBM per device.

```python
import jax
import jax.numpy as jnp
from jax import lax

D = 768
HEADS = 12
HD = 64
ROT = 16
FF = 3072
SEQ_LEN = 512
NSEQ = 16


def shard_levels(own_key, extent, shards, low, high):
    level = 1.0
    for dim, shards_of in shards:
        draws = jax.random.uniform(jax.random.fold_in(jax.random.fold_in(own_key, 6), dim), (shards_of,), jnp.float32, low / len(shards), high / len(shards))
        level = level * jnp.repeat(jnp.exp(draws), extent[dim] // shards_of).reshape((-1,) + (1,) * (len(extent) - 1 - dim))
    return level


def normal_values(rng, shape, width, most, split=(), held_as=jnp.bfloat16):
    level = shard_levels(rng, shape, split, -0.22, 0.18) if split else 1.0
    values = jax.random.normal(rng, shape, jnp.float32) * width * level
    return jnp.minimum(jnp.maximum(values, -most), most).astype(held_as)


def setup_inputs(seed: int = 0) -> dict:
    keys = jax.random.split(jax.random.key(seed), 15)
    return {
        "inputs": normal_values(keys[0], (NSEQ, SEQ_LEN, D), 1.0, 6.0, ((0, 8), (1, 4))),
        "cotangent": normal_values(keys[1], (NSEQ, SEQ_LEN, D), 1.0, 6.0, ((0, 8), (1, 4))),
        "joined_weight": normal_values(keys[2], (D, 3 * D), D ** -0.5, 0.21875, ((0, 32),)),
        "joined_bias": normal_values(keys[3], (3 * D,), 0.5, 3.0, ((0, 32),)),
        "dense_weight": normal_values(keys[4], (D, D), (D // 64) ** -0.5, 1.75, ((0, 32),)),
        "dense_bias": normal_values(keys[5], (D,), 0.5, 3.0, ((0, 32),)),
        "expand_weight": normal_values(keys[6], (D, FF), D ** -0.5, 0.21875, ((0, 32),)),
        "expand_bias": normal_values(keys[7], (FF,), 0.5, 3.0, ((0, 32),)),
        "shrink_weight": normal_values(keys[8], (FF, D), FF ** -0.5, 0.109375, ((0, 32),)),
        "shrink_bias": normal_values(keys[9], (D,), 0.5, 3.0, ((0, 32),)),
        "attn_gain": jnp.clip(1.0 + 0.1 * jax.random.normal(keys[10], (D,), jnp.float32), 0.5, 1.5).astype(jnp.bfloat16),
        "attn_shift": normal_values(keys[11], (D,), 0.5, 3.0, ((0, 32),)),
        "mlp_gain": jnp.clip(1.0 + 0.1 * jax.random.normal(keys[12], (D,), jnp.float32), 0.5, 1.5).astype(jnp.bfloat16),
        "mlp_shift": normal_values(keys[13], (D,), 0.5, 3.0, ((0, 32),)),
    }


norm_eps = 1e-05

def widen(values):
    return lax.optimization_barrier(values).astype(jnp.float32)

def layer_norm(values, gain, shift):
    mean_val = lax.optimization_barrier(jnp.mean(values, axis=-1, keepdims=True))
    centred = values - mean_val
    variance = lax.optimization_barrier(jnp.mean(centred * centred, axis=-1, keepdims=True))
    inv_std = lax.rsqrt(variance + norm_eps)
    normed = centred * inv_std
    return (normed, inv_std, normed * gain.astype(jnp.float32) + shift.astype(jnp.float32))

def norm_back(grad_out, normed, inv_std, gain):
    scaled = grad_out * gain.astype(jnp.float32)
    first = lax.optimization_barrier(jnp.mean(scaled, axis=-1, keepdims=True))
    second = lax.optimization_barrier(jnp.mean(scaled * normed, axis=-1, keepdims=True))
    return inv_std * (scaled - first - normed * second)

def rotary_tables(positions, rot_dims):
    freq = 1.0 / 10000.0 ** (jnp.arange(0, rot_dims, 2, dtype=jnp.float32) / rot_dims)
    angles = positions.astype(jnp.float32)[:, None] * freq[None, :]
    angles = jnp.concatenate([angles, angles], axis=-1)
    return (jnp.cos(angles), jnp.sin(angles))

def turn_half(part):
    half = part.shape[-1] // 2
    return jnp.concatenate([-part[..., half:], part[..., :half]], axis=-1)

def turn_half_back(part):
    half = part.shape[-1] // 2
    return jnp.concatenate([part[..., half:], -part[..., :half]], axis=-1)

def rotate_fwd(vec, cos_val, sin_val):
    rot_dims = cos_val.shape[-1]
    head_part = vec[..., :rot_dims]
    turned = head_part * cos_val + turn_half(head_part) * sin_val
    return jnp.concatenate([turned, vec[..., rot_dims:]], axis=-1)

def rotate_back(grad, cos_val, sin_val):
    rot_dims = cos_val.shape[-1]
    head_part = grad[..., :rot_dims]
    turned = head_part * cos_val + turn_half_back(head_part * sin_val)
    return jnp.concatenate([turned, grad[..., rot_dims:]], axis=-1)

def gelu_cdf(pre):
    return 0.5 * (1.0 + jax.scipy.special.erf(pre * 0.7071067811865476))

def gelu_slope(pre):
    return gelu_cdf(pre) + pre * jnp.exp(-0.5 * pre * pre) * 0.3989422804014327

def reference(inputs, cotangent, joined_weight, joined_bias, dense_weight, dense_bias, expand_weight, expand_bias, shrink_weight, shrink_bias, attn_gain, attn_shift, mlp_gain, mlp_shift):
    scale = HD ** (-0.5)
    positions = jnp.arange(SEQ_LEN, dtype=jnp.int32)
    cos_val, sin_val = rotary_tables(positions, ROT)
    cos_val = cos_val[:, None, :]
    sin_val = sin_val[:, None, :]
    allowed = positions[:, None] >= positions[None, :]

    def one_sequence(totals, pair):
        seq_in, seq_cot = pair
        rows = seq_in.astype(jnp.float32)
        normed, inv_std, affine_a = layer_norm(rows, attn_gain, attn_shift)
        affine_b = normed * mlp_gain.astype(jnp.float32) + mlp_shift.astype(jnp.float32)
        hidden_a = affine_a.astype(jnp.bfloat16)
        hidden_b = affine_b.astype(jnp.bfloat16)
        joined = jnp.dot(hidden_a, joined_weight, preferred_element_type=jnp.float32) + joined_bias.astype(jnp.float32)
        joined = joined.reshape(SEQ_LEN, HEADS, 3, HD)
        query_rot = rotate_fwd(joined[:, :, 0], cos_val, sin_val)
        key_rot = rotate_fwd(joined[:, :, 1], cos_val, sin_val)
        rotated = jnp.stack([query_rot, key_rot, joined[:, :, 2]], axis=2).astype(jnp.bfloat16)
        query_f = widen(rotated[:, :, 0])
        key_f = widen(rotated[:, :, 1])
        value_f = widen(rotated[:, :, 2])
        scores = jnp.einsum('qhd,khd->hqk', query_f, key_f) * scale
        log_total = jnp.log(lax.optimization_barrier(jnp.sum(jnp.where(allowed, jnp.exp(scores), 0.0), axis=-1)))
        probs = jnp.where(allowed, jnp.exp(scores - log_total[:, :, None]), 0.0)
        weights_f = widen(probs.astype(jnp.bfloat16))
        context = jnp.einsum('hqk,khd->qhd', weights_f, value_f)
        context_bf = context.astype(jnp.bfloat16).reshape(SEQ_LEN, D)
        attn_out = jnp.dot(context_bf, dense_weight, preferred_element_type=jnp.float32) + dense_bias.astype(jnp.float32)
        pre = jnp.dot(hidden_b, expand_weight, preferred_element_type=jnp.float32) + expand_bias.astype(jnp.float32)
        activated = (pre * gelu_cdf(pre)).astype(jnp.bfloat16)
        mlp_out = jnp.dot(activated, shrink_weight, preferred_element_type=jnp.float32) + shrink_bias.astype(jnp.float32)
        output = (rows + attn_out + mlp_out).astype(jnp.bfloat16)
        cot_f = seq_cot.astype(jnp.float32)
        out_bias_grad = lax.optimization_barrier(jnp.sum(cot_f, axis=0))
        shrink_w_grad = jnp.dot(activated.T, seq_cot, preferred_element_type=jnp.float32)
        act_grad = jnp.dot(seq_cot, shrink_weight.T, preferred_element_type=jnp.float32)
        pre_grad = act_grad * gelu_slope(pre)
        expand_b_grad = lax.optimization_barrier(jnp.sum(pre_grad, axis=0))
        pre_grad_bf = pre_grad.astype(jnp.bfloat16)
        expand_w_grad = jnp.dot(hidden_b.T, pre_grad_bf, preferred_element_type=jnp.float32)
        hidden_b_grad = jnp.dot(pre_grad_bf, expand_weight.T, preferred_element_type=jnp.float32)
        dense_w_grad = jnp.dot(context_bf.T, seq_cot, preferred_element_type=jnp.float32)
        context_grad = jnp.dot(seq_cot, dense_weight.T, preferred_element_type=jnp.float32).astype(jnp.bfloat16)
        ctx_grad_f = widen(context_grad.reshape(SEQ_LEN, HEADS, HD))
        delta = lax.optimization_barrier(jnp.sum(ctx_grad_f * context, axis=-1))
        value_grad = jnp.einsum('hqk,qhd->khd', weights_f, ctx_grad_f)
        weight_grad = jnp.einsum('qhd,khd->hqk', ctx_grad_f, value_f)
        score_grad = widen((probs * (weight_grad - delta.T[:, :, None]) * scale).astype(jnp.bfloat16))
        query_grad = rotate_back(jnp.einsum('hqk,khd->qhd', score_grad, key_f), cos_val, sin_val)
        key_grad = rotate_back(jnp.einsum('hqk,qhd->khd', score_grad, query_f), cos_val, sin_val)
        joined_grad = jnp.stack([query_grad, key_grad, value_grad], axis=2).astype(jnp.bfloat16).reshape(SEQ_LEN, 3 * D)
        joined_b_grad = lax.optimization_barrier(jnp.sum(widen(joined_grad), axis=0))
        joined_w_grad = jnp.dot(hidden_a.T, joined_grad, preferred_element_type=jnp.float32)
        hidden_a_grad = jnp.dot(joined_grad, joined_weight.T, preferred_element_type=jnp.float32)
        gain_a_grad = lax.optimization_barrier(jnp.sum(hidden_a_grad * normed, axis=0))
        shift_a_grad = lax.optimization_barrier(jnp.sum(hidden_a_grad, axis=0))
        gain_b_grad = lax.optimization_barrier(jnp.sum(hidden_b_grad * normed, axis=0))
        shift_b_grad = lax.optimization_barrier(jnp.sum(hidden_b_grad, axis=0))
        input_grad = cot_f + norm_back(hidden_a_grad, normed, inv_std, attn_gain) + norm_back(hidden_b_grad, normed, inv_std, mlp_gain)
        grads = (joined_w_grad, joined_b_grad, dense_w_grad, out_bias_grad, expand_w_grad, expand_b_grad, shrink_w_grad, out_bias_grad, gain_a_grad, shift_a_grad, gain_b_grad, shift_b_grad)
        totals = jax.tree.map(lambda left, right: left + right, totals, grads)
        return (totals, (output, input_grad))
    params = (joined_weight, joined_bias, dense_weight, dense_bias, expand_weight, expand_bias, shrink_weight, shrink_bias, attn_gain, attn_shift, mlp_gain, mlp_shift)
    start_totals = tuple((jnp.zeros(param.shape, jnp.float32) for param in params))
    totals, (outputs, input_grads) = lax.scan(one_sequence, start_totals, (inputs, cotangent))
    return (outputs, input_grads, totals[0], totals[1], totals[2], totals[3], totals[4], totals[5], totals[6], totals[7], totals[8], totals[9], totals[10], totals[11])
```

```python
import jax
import jax.numpy as jnp
from jax import lax
from jax.sharding import PartitionSpec as P

HEADS = 12
HD = 64
ROT = 16
NORM_EPS = 1e-05
BF = jnp.bfloat16
F32 = jnp.float32


def bits_of(count):
    assert count & (count - 1) == 0
    bit = 1
    out = []
    while bit < count:
        out.append(bit)
        bit *= 2
    return out


def swap(value, axis, bit):
    count = lax.axis_size(axis)
    return lax.ppermute(value, axis, [(i, i ^ bit) for i in range(count)])


def cube_gather(value, axis):
    order = [0]
    for bit in reversed(bits_of(lax.axis_size(axis))):
        value = jnp.concatenate([value, swap(value, axis, bit)], axis=0)
        order = order + [k ^ bit for k in order]
    return value, order


def cube_scatter(value, axis, wire):
    for bit in bits_of(lax.axis_size(axis)):
        half = value.shape[0] // 2
        keep, send = value[:half], value[half:]
        got = swap(send.astype(wire), axis, bit)
        value = keep.astype(F32) + got.astype(F32)
    return value


def to_natural(blocks, order, axis):
    me = lax.axis_index(axis)
    inverse = [order.index(k) for k in range(len(order))]
    ids = jnp.asarray(inverse, jnp.int32)[jnp.arange(len(order), dtype=jnp.int32) ^ me]
    return blocks[ids]


def layer_norm(values):
    mean_val = jnp.mean(values, axis=-1, keepdims=True)
    centred = values - mean_val
    variance = jnp.mean(centred * centred, axis=-1, keepdims=True)
    inv_std = lax.rsqrt(variance + NORM_EPS)
    return centred * inv_std, inv_std


def rotary_tables(positions):
    freq = 1.0 / 10000.0 ** (jnp.arange(0, ROT, 2, dtype=F32) / ROT)
    angles = positions.astype(F32)[:, None] * freq[None, :]
    angles = jnp.concatenate([angles, angles], axis=-1)
    return jnp.cos(angles), jnp.sin(angles)


def turn_half(part):
    half = part.shape[-1] // 2
    return jnp.concatenate([-part[..., half:], part[..., :half]], axis=-1)


def turn_half_back(part):
    half = part.shape[-1] // 2
    return jnp.concatenate([part[..., half:], -part[..., :half]], axis=-1)


def rotate_fwd(vec, cos_val, sin_val):
    head_part = vec[..., :ROT]
    turned = head_part * cos_val + turn_half(head_part) * sin_val
    return jnp.concatenate([turned, vec[..., ROT:]], axis=-1)


def rotate_back(grad, cos_val, sin_val):
    head_part = grad[..., :ROT]
    turned = head_part * cos_val + turn_half_back(head_part * sin_val)
    return jnp.concatenate([turned, grad[..., ROT:]], axis=-1)


def dot(left, right, dims):
    return lax.dot_general(left, right, (dims, ((), ())), preferred_element_type=F32)


def on_device(
    inputs,
    cotangent,
    joined_weight,
    joined_bias,
    dense_weight,
    dense_bias,
    expand_weight,
    expand_bias,
    shrink_weight,
    shrink_bias,
    attn_gain,
    attn_shift,
    mlp_gain,
    mlp_shift,
):
    seqs, local_len, width = inputs.shape
    sp, dp = lax.axis_size("sp"), lax.axis_size("dp")
    me = lax.axis_index("sp")
    heads = HEADS // sp
    local = seqs * local_len
    tokens = local * sp
    full_len = local_len * sp
    scale = HD ** (-0.5)
    cols = joined_weight.shape[1] // sp
    row_n = joined_weight.shape[0]
    ff_n = shrink_weight.shape[0]
    ff_all = expand_weight.shape[1]
    units = ff_all // sp

    small_parts = (
        joined_bias,
        dense_bias,
        expand_bias,
        shrink_bias,
        attn_gain,
        attn_shift,
        mlp_gain,
        mlp_shift,
    )
    sizes = [part.shape[0] for part in small_parts]
    offsets = [sum(sizes[:i]) for i in range(len(sizes))]
    small = jnp.concatenate(small_parts)[None, :]
    small, order = cube_gather(small, "sp")
    small = to_natural(small, order, "sp")[None]
    small, dp_order = cube_gather(small, "dp")
    small = to_natural(small, dp_order, "dp").astype(F32)

    def whole(index):
        return small[:, :, offsets[index] : offsets[index] + sizes[index]].reshape(-1)

    joined_add = lax.dynamic_slice_in_dim(whole(0), me * cols, cols)
    out_add = whole(1) + whole(3)
    expand_all = small[:, :, offsets[2] : offsets[2] + sizes[2]]
    expand_add = lax.dynamic_index_in_dim(expand_all, me, 1, keepdims=False).reshape(-1)
    gain_a, shift_a, gain_b, shift_b = whole(4), whole(5), whole(6), whole(7)

    expand_part = (
        expand_weight.reshape(row_n, dp, sp, ff_n).transpose(0, 2, 1, 3).reshape(row_n, ff_all)
    )
    expand_part = lax.all_to_all(expand_part, "sp", split_axis=1, concat_axis=0, tiled=True)
    joined_part = lax.all_to_all(joined_weight, "sp", split_axis=1, concat_axis=0, tiled=True)
    expand_w = lax.all_gather(expand_part, "dp", axis=0, tiled=True)
    shrink_w = lax.all_gather(shrink_weight, "dp", axis=0, tiled=True)
    joined_w = lax.all_gather(joined_part, "dp", axis=0, tiled=True)
    dense_rows = lax.all_gather(dense_weight, "dp", axis=0, tiled=True)
    dense_w = lax.all_to_all(dense_rows, "sp", split_axis=0, concat_axis=0, tiled=True)
    dense_w = dense_w.reshape(sp, dp // sp, row_n, width).transpose(1, 0, 2, 3)
    dense_w = dense_w.reshape(heads * HD, width)

    x_bf, order = cube_gather(inputs.reshape(1, local, width), "sp")
    cot_bf, _ = cube_gather(cotangent.reshape(1, local, width), "sp")
    x_bf = x_bf.reshape(tokens, width)
    cot_bf = cot_bf.reshape(tokens, width)
    normed, _ = layer_norm(x_bf.astype(F32))
    hidden_a = (normed * gain_a + shift_a).astype(BF)
    hidden_b = (normed * gain_b + shift_b).astype(BF)
    starts = jnp.asarray(order, jnp.int32) ^ me
    pos = (starts[:, None] * local_len + jnp.arange(local_len, dtype=jnp.int32)).reshape(-1)

    pre = dot(hidden_b, expand_w, ((1,), (0,))) + expand_add
    cdf = 0.5 * (1.0 + lax.erf(pre * 0.7071067811865476))
    activated = (pre * cdf).astype(BF)
    slope = cdf + pre * jnp.exp(-0.5 * pre * pre) * 0.3989422804014327
    act_grad = dot(cot_bf, shrink_w, ((1,), (1,)))
    pre_grad = act_grad * slope
    pre_grad_bf = pre_grad.astype(BF)
    expand_b_grad = jnp.sum(pre_grad, axis=0)
    expand_w_grad = dot(hidden_b, pre_grad_bf, ((0,), (0,)))
    shrink_w_grad = dot(activated, cot_bf, ((0,), (0,)))
    mlp_part = dot(activated, shrink_w, ((1,), (0,)))
    hidden_b_grad = dot(pre_grad_bf, expand_w, ((1,), (1,)))

    cos_val, sin_val = rotary_tables(pos)
    cos_val, sin_val = cos_val[:, None, None, :], sin_val[:, None, None, :]

    def by_seq(value):
        value = value.reshape(sp, seqs, local_len, value.shape[-1])
        return value.transpose(1, 0, 2, 3).reshape(seqs, full_len, -1)

    def by_block(value):
        value = value.reshape(seqs, sp, local_len, value.shape[-1])
        return value.transpose(1, 0, 2, 3).reshape(tokens, -1)

    joined = dot(by_seq(hidden_a).reshape(tokens, width), joined_w, ((1,), (0,))) + joined_add
    joined = joined.reshape(seqs, full_len, heads, 3, HD)
    cos_val = cos_val.reshape(1, full_len, 1, ROT)
    sin_val = sin_val.reshape(1, full_len, 1, ROT)
    query = rotate_fwd(joined[:, :, :, 0], cos_val, sin_val).astype(BF)
    key = rotate_fwd(joined[:, :, :, 1], cos_val, sin_val).astype(BF)
    value = joined[:, :, :, 2].astype(BF)
    scores = jnp.einsum("bqhd,bkhd->bhqk", query, key, preferred_element_type=F32) * scale
    allowed = (pos[:, None] >= pos[None, :])[None, None]
    log_total = jnp.log(
        jnp.sum(jnp.where(allowed, jnp.exp(scores), 0.0), axis=-1, keepdims=True)
    )
    probs = jnp.where(allowed, jnp.exp(scores - log_total), 0.0)
    weights = probs.astype(BF)
    context = jnp.einsum("bhqk,bkhd->bqhd", weights, value, preferred_element_type=F32)
    context_bf = by_block(context.astype(BF).reshape(seqs, full_len, heads * HD))
    attn_part = dot(context_bf, dense_w, ((1,), (0,)))
    dense_w_grad = dot(context_bf, cot_bf, ((0,), (0,)))
    context_grad = dot(cot_bf, dense_w, ((1,), (1,))).astype(BF)
    context_grad = by_seq(context_grad).reshape(seqs, full_len, heads, HD)
    delta = jnp.sum(context_grad.astype(F32) * context, axis=-1).transpose(0, 2, 1)[..., None]
    value_grad = jnp.einsum("bhqk,bqhd->bkhd", weights, context_grad, preferred_element_type=F32)
    weight_grad = jnp.einsum("bqhd,bkhd->bhqk", context_grad, value, preferred_element_type=F32)
    score_grad = (probs * (weight_grad - delta) * scale).astype(BF)
    query_grad = jnp.einsum("bhqk,bkhd->bqhd", score_grad, key, preferred_element_type=F32)
    key_grad = jnp.einsum("bhqk,bqhd->bkhd", score_grad, query, preferred_element_type=F32)
    joined_grad = jnp.stack(
        [
            rotate_back(query_grad, cos_val, sin_val),
            rotate_back(key_grad, cos_val, sin_val),
            value_grad,
        ],
        axis=3,
    ).astype(BF)
    joined_grad = by_block(joined_grad.reshape(seqs, full_len, cols))
    joined_b_grad = jnp.sum(joined_grad.astype(F32), axis=0)
    joined_w_grad = dot(hidden_a, joined_grad, ((0,), (0,)))
    hidden_a_grad = dot(joined_grad, joined_w, ((1,), (1,)))

    rows = inputs.reshape(local, width).astype(F32)
    out_sum = cube_scatter((attn_part + mlp_part).reshape(sp, local, width), "sp", BF)[0]
    output = (rows + out_sum + out_add).astype(BF).reshape(inputs.shape)
    scaled = (hidden_a_grad * gain_a + hidden_b_grad * gain_b).reshape(sp, local, width)
    scaled = cube_scatter(scaled, "sp", BF)[0]
    own_normed, own_inv = layer_norm(rows)
    first = jnp.mean(scaled, axis=-1, keepdims=True)
    second = jnp.mean(scaled * own_normed, axis=-1, keepdims=True)
    cot_f = cotangent.reshape(local, width).astype(F32)
    input_grad = cot_f + own_inv * (scaled - first - own_normed * second)
    input_grad = input_grad.reshape(inputs.shape)

    def reduce_rows(grad):
        return lax.psum_scatter(grad.astype(BF), "dp", scatter_dimension=0, tiled=True)

    expand_g = reduce_rows(expand_w_grad)
    expand_g = lax.all_to_all(expand_g, "sp", split_axis=0, concat_axis=1, tiled=True)
    expand_g = expand_g.reshape(row_n, sp, dp, ff_n).transpose(0, 2, 1, 3).reshape(row_n, ff_all)
    shrink_g = reduce_rows(shrink_w_grad)
    joined_g = reduce_rows(joined_w_grad)
    joined_g = lax.all_to_all(joined_g, "sp", split_axis=0, concat_axis=1, tiled=True)
    dense_g = dense_w_grad.astype(BF).reshape(dp // sp, sp, row_n, width).transpose(1, 0, 2, 3)
    dense_g = dense_g.reshape(heads * HD, width)
    dense_g = lax.all_to_all(dense_g, "sp", split_axis=0, concat_axis=0, tiled=True)
    dense_g = reduce_rows(dense_g)

    joined_b_all = lax.dynamic_update_slice_in_dim(
        jnp.zeros((cols * sp,), F32), joined_b_grad, me * cols, 0
    )
    mine = (jnp.arange(sp, dtype=jnp.int32) == me)[None, :, None]
    expand_b_all = jnp.where(mine, expand_b_grad.reshape(dp, 1, ff_n), 0.0)

    def split(vector):
        return vector.reshape(dp, sp, -1)

    small_grad = jnp.concatenate(
        [
            split(joined_b_all),
            expand_b_all,
            split(jnp.sum(cot_f, axis=0)),
            split(jnp.sum(hidden_a_grad * normed, axis=0)),
            split(jnp.sum(hidden_a_grad, axis=0)),
            split(jnp.sum(hidden_b_grad * normed, axis=0)),
            split(jnp.sum(hidden_b_grad, axis=0)),
        ],
        axis=2,
    )
    dp_me = lax.axis_index("dp")
    small_grad = small_grad[jnp.asarray(dp_order, jnp.int32) ^ dp_me]
    small_grad = cube_scatter(small_grad, "dp", F32)[0]
    small_grad = small_grad[jnp.asarray(order, jnp.int32) ^ me]
    small_grad = cube_scatter(small_grad, "sp", F32)[0]
    s_sizes = [sizes[0], sizes[2], sizes[1], sizes[4], sizes[5], sizes[6], sizes[7]]
    at = [sum(s_sizes[:i]) for i in range(len(s_sizes))]
    pieces = [small_grad[a : a + n] for a, n in zip(at, s_sizes)]
    joined_bg, expand_bg, out_bg, gain_ag, shift_ag, gain_bg, shift_bg = pieces
    return (
        output,
        input_grad,
        joined_g.astype(F32),
        joined_bg,
        dense_g.astype(F32),
        out_bg,
        expand_g.astype(F32),
        expand_bg,
        shrink_g.astype(F32),
        out_bg,
        gain_ag,
        shift_ag,
        gain_bg,
        shift_bg,
    )


def solution(mesh):
    token = P("dp", "sp", None)
    matrix = P(("dp", "sp"), None)
    vector = P(("dp", "sp"))
    params = (matrix, vector) * 4 + (vector,) * 4
    return jax.shard_map(
        on_device,
        mesh=mesh,
        in_specs=(token, token) + params,
        out_specs=(token, token) + params,
        check_vma=False,
    )
```

```python
import jax
import jax.numpy as jnp
from jax import lax
from jax.sharding import PartitionSpec as P

HEADS = 12
HD = 64
ROT = 16
NORM_EPS = 1e-05
BF = jnp.bfloat16
F32 = jnp.float32


def bits_of(count):
    assert count & (count - 1) == 0
    bit = 1
    out = []
    while bit < count:
        out.append(bit)
        bit *= 2
    return out


def swap(value, axis, bit):
    count = lax.axis_size(axis)
    return lax.ppermute(value, axis, [(i, i ^ bit) for i in range(count)])


def cube_gather(value, axis):
    order = [0]
    for bit in reversed(bits_of(lax.axis_size(axis))):
        value = jnp.concatenate([value, swap(value, axis, bit)], axis=0)
        order = order + [k ^ bit for k in order]
    return value, order


def cube_scatter(value, axis, wire):
    for bit in bits_of(lax.axis_size(axis)):
        half = value.shape[0] // 2
        keep, send = value[:half], value[half:]
        got = swap(send.astype(wire), axis, bit)
        value = keep.astype(F32) + got.astype(F32)
    return value


def flip_bits(blocks, axis):
    count = lax.axis_size(axis)
    me = lax.axis_index(axis)
    rest = blocks.shape[1:]
    for bit in bits_of(count):
        pairs = blocks.reshape((count // (2 * bit), 2, bit) + rest)
        blocks = jnp.where((me & bit) > 0, pairs[:, ::-1], pairs).reshape((count,) + rest)
    return blocks


def turn_bits(blocks):
    count = blocks.shape[0]
    bits = len(bits_of(count))
    rest = blocks.shape[1:]
    blocks = blocks.reshape((2,) * bits + rest)
    axes = tuple(reversed(range(bits))) + tuple(range(bits, bits + len(rest)))
    return blocks.transpose(axes).reshape((count,) + rest)


def gather_blocks(block, axis):
    blocks, _ = cube_gather(block[None], axis)
    return flip_bits(turn_bits(blocks), axis)


def scatter_blocks(blocks, axis, wire):
    return cube_scatter(turn_bits(flip_bits(blocks, axis)), axis, wire)[0]


def layer_norm(values):
    mean_val = jnp.mean(values, axis=-1, keepdims=True)
    centred = values - mean_val
    variance = jnp.mean(centred * centred, axis=-1, keepdims=True)
    inv_std = lax.rsqrt(variance + NORM_EPS)
    return centred * inv_std, inv_std


def rotary_tables(positions):
    freq = 1.0 / 10000.0 ** (jnp.arange(0, ROT, 2, dtype=F32) / ROT)
    angles = positions.astype(F32)[:, None] * freq[None, :]
    angles = jnp.concatenate([angles, angles], axis=-1)
    return jnp.cos(angles), jnp.sin(angles)


def turn_half(part):
    half = part.shape[-1] // 2
    return jnp.concatenate([-part[..., half:], part[..., :half]], axis=-1)


def turn_half_back(part):
    half = part.shape[-1] // 2
    return jnp.concatenate([part[..., half:], -part[..., :half]], axis=-1)


def rotate_fwd(vec, cos_val, sin_val):
    head_part = vec[..., :ROT]
    turned = head_part * cos_val + turn_half(head_part) * sin_val
    return jnp.concatenate([turned, vec[..., ROT:]], axis=-1)


def rotate_back(grad, cos_val, sin_val):
    head_part = grad[..., :ROT]
    turned = head_part * cos_val + turn_half_back(head_part * sin_val)
    return jnp.concatenate([turned, grad[..., ROT:]], axis=-1)


def dot(left, right, dims):
    return lax.dot_general(left, right, (dims, ((), ())), preferred_element_type=F32)


def on_device(
    inputs,
    cotangent,
    joined_weight,
    joined_bias,
    dense_weight,
    dense_bias,
    expand_weight,
    expand_bias,
    shrink_weight,
    shrink_bias,
    attn_gain,
    attn_shift,
    mlp_gain,
    mlp_shift,
):
    seqs, local_len, width = inputs.shape
    sp, dp = lax.axis_size("sp"), lax.axis_size("dp")
    me = lax.axis_index("sp")
    heads = HEADS // sp
    local = seqs * local_len
    tokens = local * sp
    full_len = local_len * sp
    scale = HD ** (-0.5)
    cols = joined_weight.shape[1] // sp
    row_n = joined_weight.shape[0]
    ff_n = shrink_weight.shape[0]
    ff_all = expand_weight.shape[1]
    units = ff_all // sp

    small_parts = (
        joined_bias,
        dense_bias,
        expand_bias,
        shrink_bias,
        attn_gain,
        attn_shift,
        mlp_gain,
        mlp_shift,
    )
    sizes = [part.shape[0] for part in small_parts]
    offsets = [sum(sizes[:i]) for i in range(len(sizes))]
    total = sum(sizes)
    small = jnp.concatenate(small_parts + (jnp.zeros((8 * width - total,), BF),))

    x_own = jnp.concatenate([inputs.reshape(local, width), small.reshape(8, width)])[None]
    x_all, order = cube_gather(x_own, "sp")
    x_bf = x_all[:, :local].reshape(tokens, width)
    cot_bf, _ = cube_gather(cotangent.reshape(1, local, width), "sp")
    cot_bf = cot_bf.reshape(tokens, width)
    small = flip_bits(turn_bits(x_all[:, local:].reshape(sp, 8 * width)[:, :total]), "sp")
    extra = -(-sp * total // width // 8) * 8
    small = jnp.concatenate([small.reshape(-1), jnp.zeros((extra * width - sp * total,), BF)])

    expand_part = (
        expand_weight.reshape(row_n, dp, sp, ff_n).transpose(0, 2, 1, 3).reshape(row_n, ff_all)
    )
    expand_part = lax.all_to_all(expand_part, "sp", split_axis=1, concat_axis=0, tiled=True)
    joined_part = lax.all_to_all(joined_weight, "sp", split_axis=1, concat_axis=0, tiled=True)
    rows_d = row_n * sp
    dense_part = dense_weight.reshape(rows_d, width // sp)
    attn_pack = jnp.concatenate([joined_part, dense_part], axis=1)
    attn_pack = jnp.concatenate([attn_pack, small.reshape(extra, width)], axis=0)
    attn_all = gather_blocks(attn_pack, "dp")
    expand_w = gather_blocks(expand_part, "dp").reshape(dp * rows_d, units)
    shrink_w = gather_blocks(shrink_weight, "dp").reshape(units, width)
    joined_w = attn_all[:, :rows_d, :cols].reshape(dp * rows_d, cols)
    dense_rows = attn_all[:, :rows_d, cols:].reshape(dp * row_n, width)
    dense_w = lax.all_to_all(dense_rows, "sp", split_axis=0, concat_axis=0, tiled=True)
    dense_w = dense_w.reshape(sp, dp // sp, row_n, width).transpose(1, 0, 2, 3)
    dense_w = dense_w.reshape(heads * HD, width)

    small = attn_all[:, rows_d:].reshape(dp, extra * width)[:, : sp * total]
    small = small.reshape(dp, sp, total).astype(F32)

    def whole(index):
        return small[:, :, offsets[index] : offsets[index] + sizes[index]].reshape(-1)

    joined_add = lax.dynamic_slice_in_dim(whole(0), me * cols, cols)
    out_add = whole(1) + whole(3)
    expand_all = small[:, :, offsets[2] : offsets[2] + sizes[2]]
    expand_add = lax.dynamic_index_in_dim(expand_all, me, 1, keepdims=False).reshape(-1)
    gain_a, shift_a, gain_b, shift_b = whole(4), whole(5), whole(6), whole(7)

    normed, _ = layer_norm(x_bf.astype(F32))
    hidden_a = (normed * gain_a + shift_a).astype(BF)
    hidden_b = (normed * gain_b + shift_b).astype(BF)
    starts = jnp.asarray(order, jnp.int32) ^ me
    pos = (starts[:, None] * local_len + jnp.arange(local_len, dtype=jnp.int32)).reshape(-1)

    pre = dot(hidden_b, expand_w, ((1,), (0,))) + expand_add
    cdf = 0.5 * (1.0 + lax.erf(pre * 0.7071067811865476))
    activated = (pre * cdf).astype(BF)
    slope = cdf + pre * jnp.exp(-0.5 * pre * pre) * 0.3989422804014327
    act_grad = dot(cot_bf, shrink_w, ((1,), (1,)))
    pre_grad = act_grad * slope
    pre_grad_bf = pre_grad.astype(BF)
    expand_b_grad = jnp.sum(pre_grad, axis=0)
    expand_w_grad = dot(hidden_b, pre_grad_bf, ((0,), (0,)))
    shrink_w_grad = dot(activated, cot_bf, ((0,), (0,)))
    mlp_part = dot(activated, shrink_w, ((1,), (0,)))
    hidden_b_grad = dot(pre_grad_bf, expand_w, ((1,), (1,)))

    cos_val, sin_val = rotary_tables(pos)
    cos_val, sin_val = cos_val[:, None, None, :], sin_val[:, None, None, :]

    def by_seq(value):
        value = value.reshape(sp, seqs, local_len, value.shape[-1])
        return value.transpose(1, 0, 2, 3).reshape(seqs, full_len, -1)

    def by_block(value):
        value = value.reshape(seqs, sp, local_len, value.shape[-1])
        return value.transpose(1, 0, 2, 3).reshape(tokens, -1)

    joined = dot(by_seq(hidden_a).reshape(tokens, width), joined_w, ((1,), (0,))) + joined_add
    joined = joined.reshape(seqs, full_len, heads, 3, HD)
    cos_val = cos_val.reshape(1, full_len, 1, ROT)
    sin_val = sin_val.reshape(1, full_len, 1, ROT)
    query = rotate_fwd(joined[:, :, :, 0], cos_val, sin_val).astype(BF)
    key = rotate_fwd(joined[:, :, :, 1], cos_val, sin_val).astype(BF)
    value = joined[:, :, :, 2].astype(BF)
    scores = jnp.einsum("bqhd,bkhd->bhqk", query, key, preferred_element_type=F32) * scale
    allowed = (pos[:, None] >= pos[None, :])[None, None]
    log_total = jnp.log(
        jnp.sum(jnp.where(allowed, jnp.exp(scores), 0.0), axis=-1, keepdims=True)
    )
    probs = jnp.where(allowed, jnp.exp(scores - log_total), 0.0)
    weights = probs.astype(BF)
    context = jnp.einsum("bhqk,bkhd->bqhd", weights, value, preferred_element_type=F32)
    context_bf = by_block(context.astype(BF).reshape(seqs, full_len, heads * HD))
    attn_part = dot(context_bf, dense_w, ((1,), (0,)))
    dense_w_grad = dot(context_bf, cot_bf, ((0,), (0,)))
    context_grad = dot(cot_bf, dense_w, ((1,), (1,))).astype(BF)
    context_grad = by_seq(context_grad).reshape(seqs, full_len, heads, HD)
    delta = jnp.sum(context_grad.astype(F32) * context, axis=-1).transpose(0, 2, 1)[..., None]
    value_grad = jnp.einsum("bhqk,bqhd->bkhd", weights, context_grad, preferred_element_type=F32)
    weight_grad = jnp.einsum("bqhd,bkhd->bhqk", context_grad, value, preferred_element_type=F32)
    score_grad = (probs * (weight_grad - delta) * scale).astype(BF)
    query_grad = jnp.einsum("bhqk,bkhd->bqhd", score_grad, key, preferred_element_type=F32)
    key_grad = jnp.einsum("bhqk,bqhd->bkhd", score_grad, query, preferred_element_type=F32)
    joined_grad = jnp.stack(
        [
            rotate_back(query_grad, cos_val, sin_val),
            rotate_back(key_grad, cos_val, sin_val),
            value_grad,
        ],
        axis=3,
    ).astype(BF)
    joined_grad = by_block(joined_grad.reshape(seqs, full_len, cols))
    joined_b_grad = jnp.sum(joined_grad.astype(F32), axis=0)
    joined_w_grad = dot(hidden_a, joined_grad, ((0,), (0,)))
    hidden_a_grad = dot(joined_grad, joined_w, ((1,), (1,)))

    rows = inputs.reshape(local, width).astype(F32)
    out_sum = cube_scatter((attn_part + mlp_part).reshape(sp, local, width), "sp", BF)[0]
    output = (rows + out_sum + out_add).astype(BF).reshape(inputs.shape)
    scaled = (hidden_a_grad * gain_a + hidden_b_grad * gain_b).reshape(sp, local, width)
    scaled = cube_scatter(scaled, "sp", BF)[0]
    own_normed, own_inv = layer_norm(rows)
    first = jnp.mean(scaled, axis=-1, keepdims=True)
    second = jnp.mean(scaled * own_normed, axis=-1, keepdims=True)
    cot_f = cotangent.reshape(local, width).astype(F32)
    input_grad = cot_f + own_inv * (scaled - first - own_normed * second)
    input_grad = input_grad.reshape(inputs.shape)

    joined_b_all = lax.dynamic_update_slice_in_dim(
        jnp.zeros((cols * sp,), F32), joined_b_grad, me * cols, 0
    )
    mine = (jnp.arange(sp, dtype=jnp.int32) == me)[None, :, None]
    expand_b_all = jnp.where(mine, expand_b_grad.reshape(dp, 1, ff_n), 0.0)

    def split(vector):
        return vector.reshape(dp, sp, -1)

    small_grad = jnp.concatenate(
        [
            split(joined_b_all),
            expand_b_all,
            split(jnp.sum(cot_f, axis=0)),
            split(jnp.sum(hidden_a_grad * normed, axis=0)),
            split(jnp.sum(hidden_a_grad, axis=0)),
            split(jnp.sum(hidden_b_grad * normed, axis=0)),
            split(jnp.sum(hidden_b_grad, axis=0)),
        ],
        axis=2,
    )

    s_total = small_grad.shape[2]
    extra = -(-sp * s_total // width // 8) * 8
    small_grad = small_grad.reshape(dp, sp * s_total)
    small_grad = jnp.pad(small_grad, ((0, 0), (0, extra * width - sp * s_total)))
    small_grad = small_grad.reshape(dp, extra, width)
    dense_g = dense_w_grad.astype(BF).reshape(dp // sp, sp, row_n, width).transpose(1, 0, 2, 3)
    dense_g = dense_g.reshape(heads * HD, width)
    dense_g = lax.all_to_all(dense_g, "sp", split_axis=0, concat_axis=0, tiled=True)
    attn_g = jnp.concatenate(
        [
            joined_w_grad.astype(BF).reshape(dp, rows_d, cols),
            dense_g.reshape(dp, rows_d, width // sp),
        ],
        axis=2,
    )
    attn_g = scatter_blocks(attn_g, "dp", BF)
    dense_g = attn_g[:, cols:].reshape(row_n, width)
    joined_g = attn_g[:, :cols].astype(BF)
    joined_g = lax.all_to_all(joined_g, "sp", split_axis=0, concat_axis=1, tiled=True)
    expand_g = jnp.concatenate([expand_w_grad.reshape(dp, rows_d, units), small_grad], axis=1)
    expand_g = scatter_blocks(expand_g, "dp", BF)
    small_grad = expand_g[rows_d:].reshape(-1)[: sp * s_total].reshape(sp, s_total)
    small_grad = scatter_blocks(small_grad, "sp", F32)
    expand_g = expand_g[:rows_d].astype(BF)
    expand_g = lax.all_to_all(expand_g, "sp", split_axis=0, concat_axis=1, tiled=True)
    expand_g = expand_g.reshape(row_n, sp, dp, ff_n).transpose(0, 2, 1, 3).reshape(row_n, ff_all)
    shrink_g = scatter_blocks(shrink_w_grad.reshape(dp, ff_n, width), "dp", BF)
    s_sizes = [sizes[0], sizes[2], sizes[1], sizes[4], sizes[5], sizes[6], sizes[7]]
    at = [sum(s_sizes[:i]) for i in range(len(s_sizes))]
    pieces = [small_grad[a : a + n] for a, n in zip(at, s_sizes)]
    joined_bg, expand_bg, out_bg, gain_ag, shift_ag, gain_bg, shift_bg = pieces
    return (
        output,
        input_grad,
        joined_g.astype(F32),
        joined_bg,
        dense_g.astype(F32),
        out_bg,
        expand_g.astype(F32),
        expand_bg,
        shrink_g.astype(F32),
        out_bg,
        gain_ag,
        shift_ag,
        gain_bg,
        shift_bg,
    )


def solution(mesh):
    token = P("dp", "sp", None)
    matrix = P(("dp", "sp"), None)
    vector = P(("dp", "sp"))
    params = (matrix, vector) * 4 + (vector,) * 4
    return jax.shard_map(
        on_device,
        mesh=mesh,
        in_specs=(token, token) + params,
        out_specs=(token, token) + params,
        check_vma=False,
    )
```

```python
import functools

import jax
import jax.numpy as jnp
from jax import lax
from jax.experimental import pallas as pl
from jax.experimental.pallas import tpu as pltpu
from jax.sharding import PartitionSpec as P

HEADS = 12
HD = 64
ROT = 16
LANES = 128
NORM_EPS = 1e-05
BF = jnp.bfloat16
F32 = jnp.float32
VMEM_LIMIT = 60 * 1024 * 1024


def bits_of(count):
    assert count & (count - 1) == 0
    bit = 1
    out = []
    while bit < count:
        out.append(bit)
        bit *= 2
    return out


def cube_order(count):
    order = [0]
    for bit in reversed(bits_of(count)):
        order = order + [k ^ bit for k in order]
    return order


def swap(value, axis, bit):
    count = lax.axis_size(axis)
    return lax.ppermute(value, axis, [(i, i ^ bit) for i in range(count)])


def halves(block, axis):
    mine, got = None, block[None]
    for bit in reversed(bits_of(lax.axis_size(axis))):
        mine = got if mine is None else jnp.concatenate([mine, got], axis=0)
        got = swap(mine, axis, bit)
    return mine, got


def token_blocks(block, axis):
    blocks = [block]
    for bit in reversed(bits_of(lax.axis_size(axis))):
        blocks = blocks + [swap(b, axis, bit) for b in blocks]
    return blocks


def cube_scatter(value, axis, wire):
    for bit in bits_of(lax.axis_size(axis)):
        half = value.shape[0] // 2
        got = swap(value[half:].astype(wire), axis, bit)
        value = value[:half].astype(F32) + got.astype(F32)
    return value


def flip_bits(blocks, axis):
    count = lax.axis_size(axis)
    me = lax.axis_index(axis)
    rest = blocks.shape[1:]
    for bit in bits_of(count):
        pairs = blocks.reshape((count // (2 * bit), 2, bit) + rest)
        blocks = jnp.where((me & bit) > 0, pairs[:, ::-1], pairs).reshape((count,) + rest)
    return blocks


def turn_bits(blocks):
    count = blocks.shape[0]
    bits = len(bits_of(count))
    rest = blocks.shape[1:]
    blocks = blocks.reshape((2,) * bits + rest)
    axes = tuple(reversed(range(bits))) + tuple(range(bits, bits + len(rest)))
    return blocks.transpose(axes).reshape((count,) + rest)


def layer_norm(values):
    mean_val = jnp.mean(values, axis=-1, keepdims=True)
    centred = values - mean_val
    variance = jnp.mean(centred * centred, axis=-1, keepdims=True)
    inv_std = lax.rsqrt(variance + NORM_EPS)
    return centred * inv_std, inv_std


def dot(left, right, left_dim, right_dim):
    dims = (((left_dim,), (right_dim,)), ((), ()))
    return lax.dot_general(left, right, dims, preferred_element_type=F32)


def row_sum(value):
    return jnp.sum(value, axis=0, keepdims=True)


def copies_in(blocks, target, rows, sem):
    out = []
    for i, block in enumerate(blocks):
        out.append(pltpu.make_async_copy(block, target.at[pl.ds(i * rows, rows)], sem.at[i]))
    return out


def placed(ids, mine, got, target, rows, width, sem):
    out = []
    half = mine.shape[0]
    for p in range(2 * half):
        source = mine.at[p] if p < half else got.at[p - half]
        if source.shape != (rows, width):
            source = source.at[pl.ds(0, rows), pl.ds(0, width)]
        to = pl.multiple_of(ids[p] * rows, 8)
        out.append(pltpu.make_async_copy(source, target.at[pl.ds(to, rows)], sem.at[p]))
    return out


def sent(ids, source, out, rows, sem):
    todo = []
    for p in range(out.shape[0]):
        at = pl.multiple_of(ids[p] * rows, 8)
        to = out.at[p] if out.shape[1] == rows else out.at[p, pl.ds(0, rows)]
        todo.append(pltpu.make_async_copy(source.at[pl.ds(at, rows)], to, sem.at[p]))
    return todo


def run(copies):
    for copy in copies:
        copy.start()


def finish(copies):
    for copy in copies:
        copy.wait()


def grad_rows(left, right, out):
    rows = 256

    @pl.loop(0, left.shape[1] // rows)
    def _(r):
        at = pl.ds(pl.multiple_of(r * rows, rows), rows)
        out[at, :] = dot(left[:, at], right[...], 0, 0).astype(BF)


def mlp_kernel(sp, ids, *refs):
    xs, cots = refs[:sp], refs[sp : 2 * sp]
    ew_mine, ew_got, sw_mine, sw_got, ap, ea, vec, dense = refs[2 * sp : 2 * sp + 8]
    eg_out, sg_out, keep, send, sums = refs[2 * sp + 8 : 2 * sp + 13]
    x, cot, ew, sw, hid, act, pgr, eg, sg, sem = refs[2 * sp + 13 :]
    width = x.shape[1]
    chunk = x.shape[0] // sp
    rows = ew_mine.shape[1]
    units = sw_mine.shape[1]
    gets = (
        copies_in([b.at[pl.ds(0, chunk)] for b in xs], x, chunk, sem.at[0])
        + copies_in(cots, cot, chunk, sem.at[1])
        + placed(ids, ew_mine, ew_got, ew, rows, ew.shape[1], sem.at[2])
        + placed(ids, sw_mine, sw_got, sw, units, width, sem.at[3])
    )
    run(gets)
    sums[...] = jnp.zeros_like(sums)
    finish(gets)
    gain, shift, add = vec[0:1, :], vec[1:2, :], vec[2:3, : ew.shape[1]]

    @pl.loop(0, sp)
    def _(k):
        at = pl.ds(pl.multiple_of(k * chunk, chunk), chunk)
        normed, _ = layer_norm(x[at, :].astype(F32))
        hidden = (normed * gain + shift).astype(BF)
        hid[at, :] = hidden
        pre = dot(hidden, ew[...], 1, 0) + add
        cdf = 0.5 * (1.0 + lax.erf(pre * 0.7071067811865476))
        activated = (pre * cdf).astype(BF)
        act[at, :] = activated
        slope = cdf + pre * jnp.exp(-0.5 * pre * pre) * 0.3989422804014327
        pre_grad = dot(cot[at, :], sw[...], 1, 1) * slope
        sums[0:1, : ew.shape[1]] += row_sum(pre_grad)
        pre_grad_bf = pre_grad.astype(BF)
        pgr[at, :] = pre_grad_bf
        out_part = dot(activated, sw[...], 1, 0) + ap[k].astype(F32)
        hidden_grad = dot(pre_grad_bf, ew[...], 1, 1)
        sums[1:2, :] += row_sum(hidden_grad * normed)
        sums[2:3, :] += row_sum(hidden_grad)
        scaled = hidden_grad * gain + ea[k].astype(F32)

        @pl.when(k < sp // 2)
        def _():
            keep[k, 0] = out_part.astype(BF)
            keep[k, 1] = scaled.astype(BF)

        @pl.when(k >= sp // 2)
        def _():
            send[k - sp // 2, 0] = out_part.astype(BF)
            send[k - sp // 2, 1] = scaled.astype(BF)

    grad_rows(hid, pgr, eg)
    puts = sent(ids, eg, eg_out, rows, sem.at[0])
    run(puts)
    grad_rows(act, cot, sg)
    more = sent(ids, sg, sg_out, units, sem.at[1])
    for p in range(sg_out.shape[0]):
        to = sg_out.at[p, pl.ds(units, dense.shape[1])]
        more.append(pltpu.make_async_copy(dense.at[ids[p]], to, sem.at[2, p]))
    run(more)
    finish(puts + more)


def attn_kernel(sp, seqs, heads, ids, *refs):
    xs, cots = refs[:sp], refs[sp : 2 * sp]
    jw_mine, jw_got, dw, vec, jadd, cos_ref, sin_ref, posc, posr = refs[2 * sp : 2 * sp + 9]
    ap, ea, jg_out, dense_g, sums, jsum = refs[2 * sp + 9 : 2 * sp + 15]
    x, cot, jw, hid, rot, cg, ctx, jgf, jgb, ctk, gr, sem = refs[2 * sp + 15 :]
    width = x.shape[1]
    wide = jw.shape[1]
    cols = heads * 3 * HD
    chunk = x.shape[0] // sp
    part = chunk // seqs
    full = part * sp
    rows = jg_out.shape[1]
    scale = HD ** (-0.5)
    gets = (
        copies_in([b.at[pl.ds(0, chunk)] for b in xs], x, chunk, sem.at[0])
        + copies_in(cots, cot, chunk, sem.at[1])
        + placed(ids, jw_mine, jw_got, jw, rows, wide, sem.at[2])
    )
    run(gets)
    sums[...] = jnp.zeros_like(sums)
    jsum[...] = jnp.zeros_like(jsum)
    jgf[:, cols:] = jnp.zeros((jgf.shape[0], wide - cols), F32)
    finish(gets)
    gain, shift = vec[0:1, :], vec[1:2, :]

    def tables(g, k):
        at = pl.ds(pl.multiple_of(k * part, part), part)
        lane = lax.broadcasted_iota(jnp.int32, (part, LANES), 1)
        col = lane + g * LANES
        inner = col % HD
        turned = (inner < ROT) & ((col // HD) % 3 < 2) & (col < cols)
        cos_val, sin_val = cos_ref[at, :], sin_ref[at, :]
        low = jnp.where(turned & (inner < ROT // 2), sin_val, 0.0)
        high = jnp.where(turned & (inner >= ROT // 2), sin_val, 0.0)
        both = [jnp.where(turned, cos_val, 1.0), low, high]
        return [jnp.concatenate([t] * seqs, axis=0) for t in both]

    def rotate(value, g, k, sign):
        cos_val, low, high = tables(g, k)
        up = pltpu.roll(value, LANES - ROT // 2, 1)
        down = pltpu.roll(value, ROT // 2, 1)
        return value * cos_val + sign * (down * high - up * low)

    def spread(ref, k, lanes, value):
        for b in range(seqs):
            at = pl.ds(pl.multiple_of(b * full + k * part, part), part)
            ref[at, lanes] = value[b * part : (b + 1) * part]

    def collect(ref, k, lanes):
        at = [pl.ds(pl.multiple_of(b * full + k * part, part), part) for b in range(seqs)]
        return jnp.concatenate([ref[a, lanes] for a in at], axis=0)

    @pl.loop(0, sp)
    def _(k):
        at = pl.ds(pl.multiple_of(k * chunk, chunk), chunk)
        normed, _ = layer_norm(x[at, :].astype(F32))
        hidden = (normed * gain + shift).astype(BF)
        hid[at, :] = hidden
        joined = dot(hidden, jw[...], 1, 0) + jadd[...]
        for g in range(wide // LANES):
            lanes = slice(g * LANES, (g + 1) * LANES)
            spread(rot, k, lanes, rotate(joined[:, lanes], g, k, 1.0).astype(BF))
        spread(cg, k, slice(None), dot(cot[at, :], dw[...], 1, 1).astype(BF))

    allowed = posc[...] >= posr[...]

    @pl.loop(0, seqs)
    def _(b):
        at = pl.ds(pl.multiple_of(b * full, full), full)
        for h in range(heads):
            q0 = h * 3 * HD
            query = rot[at, q0 : q0 + HD]
            key = rot[at, q0 + HD : q0 + 2 * HD]
            value = rot[at, q0 + 2 * HD : q0 + 3 * HD]
            grad = cg[at, h * HD : (h + 1) * HD]
            scores = dot(query, key, 1, 1) * scale
            total = jnp.sum(jnp.where(allowed, jnp.exp(scores), 0.0), axis=-1, keepdims=True)
            probs = jnp.where(allowed, jnp.exp(scores - jnp.log(total)), 0.0)
            weights = probs.astype(BF)
            context = dot(weights, value, 1, 0)
            ctx[at, h * HD : (h + 1) * HD] = context.astype(BF)
            delta = jnp.sum(grad.astype(F32) * context, axis=-1, keepdims=True)
            jgf[at, q0 + 2 * HD : q0 + 3 * HD] = dot(weights, grad, 0, 0)
            score_grad = (probs * (dot(grad, value, 1, 1) - delta) * scale).astype(BF)
            jgf[at, q0 : q0 + HD] = dot(score_grad, key, 1, 0)
            jgf[at, q0 + HD : q0 + 2 * HD] = dot(score_grad, query, 0, 0)

    @pl.loop(0, sp)
    def _(k):
        at = pl.ds(pl.multiple_of(k * chunk, chunk), chunk)
        for g in range(wide // LANES):
            lanes = slice(g * LANES, (g + 1) * LANES)
            back = rotate(collect(jgf, k, lanes), g, k, -1.0).astype(BF)
            jgb[at, lanes] = back
            jsum[0:1, lanes] += row_sum(back.astype(F32))
        hidden_grad = dot(jgb[at, :], jw[...], 1, 1)
        normed, _ = layer_norm(x[at, :].astype(F32))
        sums[0:1, :] += row_sum(hidden_grad * normed)
        sums[1:2, :] += row_sum(hidden_grad)
        ea[k] = (hidden_grad * gain).astype(BF)
        context = collect(ctx, k, slice(None))
        ctk[at, :] = context
        ap[k] = dot(context, dw[...], 1, 0).astype(BF)

    grad_rows(hid, jgb, gr)
    puts = sent(ids, gr, jg_out, rows, sem.at[0])
    run(puts)
    dense_g[...] = dot(ctk[...], cot[...], 0, 0).astype(BF)
    finish(puts)


ANY = pl.BlockSpec(memory_space=pl.ANY)
IN_VMEM = pl.BlockSpec(memory_space=pltpu.VMEM)
IN_SMEM = pl.BlockSpec(memory_space=pltpu.SMEM)


def call(body, name, args, specs, outs, out_specs, scratch, flops):
    moved = sum(a.size * a.dtype.itemsize for a in args)
    moved += sum(o.size * o.dtype.itemsize for o in outs)
    return pl.pallas_call(
        body,
        name=name,
        in_specs=specs,
        out_shape=outs,
        out_specs=out_specs,
        scratch_shapes=scratch,
        compiler_params=pltpu.CompilerParams(vmem_limit_bytes=VMEM_LIMIT),
        cost_estimate=pl.CostEstimate(flops=flops, bytes_accessed=moved, transcendentals=0),
    )(*args)


def attention(ids, xs, cots, jw, dw, vec, jadd, tables, poss, seqs, heads):
    sp = len(xs)
    chunk, width = cots[0].shape
    tokens = sp * chunk
    wide = jadd.shape[1]
    dp = 2 * jw[0].shape[0]
    rows = width // dp
    shape = jax.ShapeDtypeStruct
    outs = [
        shape((sp, chunk, width), BF),
        shape((sp, chunk, width), BF),
        shape((dp, rows, wide), BF),
        shape((heads * HD, width), BF),
        shape((8, width), F32),
        shape((8, wide), F32),
    ]
    scratch = [
        pltpu.VMEM((tokens, width), BF),
        pltpu.VMEM((tokens, width), BF),
        pltpu.VMEM((width, wide), BF),
        pltpu.VMEM((tokens, width), BF),
        pltpu.VMEM((tokens, wide), BF),
        pltpu.VMEM((tokens, heads * HD), BF),
        pltpu.VMEM((tokens, heads * HD), BF),
        pltpu.VMEM((tokens, wide), F32),
        pltpu.VMEM((tokens, wide), BF),
        pltpu.VMEM((tokens, heads * HD), BF),
        pltpu.VMEM((width, wide), BF),
        pltpu.SemaphoreType.DMA((3, max(dp, sp))),
    ]
    return call(
        functools.partial(attn_kernel, sp, seqs, heads),
        "attention_branch",
        [ids, *xs, *cots, *jw, dw, vec, jadd, *tables, *poss],
        [IN_SMEM] + [ANY] * (2 * sp + 2) + [IN_VMEM] * 7,
        outs,
        [IN_VMEM, IN_VMEM, ANY, IN_VMEM, IN_VMEM, IN_VMEM],
        scratch,
        12 * tokens * width * wide,
    )


def feed_forward(ids, xs, cots, ew, sw, ap, ea, vec, dense):
    sp = len(xs)
    chunk, width = cots[0].shape
    tokens = sp * chunk
    units = ew[0].shape[2]
    dp = 2 * ew[0].shape[0]
    rows, per, extra = ew[0].shape[1], sw[0].shape[1], dense.shape[1]
    shape = jax.ShapeDtypeStruct
    outs = [
        shape((dp, rows, units), BF),
        shape((dp, per + extra + 8, width), BF),
        shape((sp // 2, 2, chunk, width), BF),
        shape((sp // 2, 2, chunk, width), BF),
        shape((8, width), F32),
    ]
    scratch = [
        pltpu.VMEM((tokens, width), BF),
        pltpu.VMEM((tokens, width), BF),
        pltpu.VMEM((width, units), BF),
        pltpu.VMEM((units, width), BF),
        pltpu.VMEM((tokens, width), BF),
        pltpu.VMEM((tokens, units), BF),
        pltpu.VMEM((tokens, units), BF),
        pltpu.VMEM((width, units), BF),
        pltpu.VMEM((units, width), BF),
        pltpu.SemaphoreType.DMA((4, max(dp, sp))),
    ]
    return call(
        functools.partial(mlp_kernel, sp),
        "feed_forward_branch",
        [ids, *xs, *cots, *ew, *sw, ap, ea, vec, dense],
        [IN_SMEM] + [ANY] * (2 * sp + 4) + [IN_VMEM] * 4,
        outs,
        [ANY, ANY, IN_VMEM, IN_VMEM, IN_VMEM],
        scratch,
        12 * tokens * width * units,
    )


def on_device(
    inputs,
    cotangent,
    joined_weight,
    joined_bias,
    dense_weight,
    dense_bias,
    expand_weight,
    expand_bias,
    shrink_weight,
    shrink_bias,
    attn_gain,
    attn_shift,
    mlp_gain,
    mlp_shift,
):
    seqs, local_len, width = inputs.shape
    sp, dp = lax.axis_size("sp"), lax.axis_size("dp")
    me, dp_me = lax.axis_index("sp"), lax.axis_index("dp")
    heads = HEADS // sp
    local = seqs * local_len
    cols = joined_weight.shape[1] // sp
    wide = -(-cols // LANES) * LANES
    row_n = joined_weight.shape[0]
    rows_d = row_n * sp
    ff_n = shrink_weight.shape[0]
    units = ff_n * dp
    sp_order, dp_order = cube_order(sp), cube_order(dp)
    ids = jnp.asarray(dp_order, jnp.int32) ^ dp_me

    expand_part = expand_weight.reshape(row_n, dp, sp, ff_n).transpose(2, 0, 1, 3)
    joined_part = joined_weight.reshape(row_n, sp, cols).transpose(1, 0, 2)
    joined_part = jnp.pad(joined_part, ((0, 0), (0, 0), (0, units - cols)))
    both = jnp.concatenate([expand_part.reshape(sp, row_n, units), joined_part], axis=1)
    both = lax.all_to_all(both, "sp", split_axis=0, concat_axis=0, tiled=True)
    expand_part = both[:, :row_n].reshape(rows_d, units)
    joined_part = both[:, row_n:, :cols].reshape(rows_d, cols)

    small_parts = (
        joined_bias,
        dense_bias,
        expand_bias,
        shrink_bias,
        attn_gain,
        attn_shift,
        mlp_gain,
        mlp_shift,
    )
    sizes = [part.shape[0] for part in small_parts]
    small = jnp.stack([jnp.pad(part, (0, width - part.shape[0])) for part in small_parts])
    xs = token_blocks(jnp.concatenate([inputs.reshape(local, width), small]), "sp")
    cots = token_blocks(cotangent.reshape(local, width), "sp")
    small = jnp.stack([block[local:, :LANES] for block in xs])
    small = flip_bits(turn_bits(small), "sp").transpose(1, 0, 2).reshape(8, sp * LANES)
    small = jnp.pad(small, ((0, 0), (0, width - sp * LANES)))

    dense_part = dense_weight.reshape(rows_d, width // sp)
    attn_pack = jnp.concatenate([joined_part, dense_part], axis=1)
    attn_pack = jnp.concatenate([attn_pack, small], axis=0)
    joined_w = halves(attn_pack, "dp")
    shrink_w = halves(shrink_weight, "dp")
    expand_w = halves(expand_part, "dp")

    def natural(lanes_at, lanes, rows_at, rows):
        got = [h[:, rows_at : rows_at + rows, lanes_at : lanes_at + lanes] for h in joined_w]
        return flip_bits(turn_bits(jnp.concatenate(got, axis=0)), "dp")

    dense_rows = natural(cols, width // sp, 0, rows_d).reshape(sp, dp // sp, rows_d, width // sp)
    dense_w = lax.all_to_all(dense_rows, "sp", split_axis=0, concat_axis=0, tiled=True)
    dense_w = dense_w.transpose(1, 0, 2, 3).reshape(heads * HD, width)
    small = natural(0, sp * LANES, rows_d, 8).reshape(dp, 8, sp, LANES).astype(F32)

    def whole(index):
        return small[:, index, :, : sizes[index]].reshape(-1)

    joined_add = lax.dynamic_slice_in_dim(whole(0), me * cols, cols)
    out_add = whole(1) + whole(3)
    expand_add = lax.dynamic_index_in_dim(small[:, 2], me, 1, keepdims=False)[:, : sizes[2]]

    def stacked(vectors):
        vectors = [jnp.pad(v.reshape(-1), (0, width - v.size)) for v in vectors]
        return jnp.stack(vectors + [jnp.zeros((width,), F32)] * (8 - len(vectors)))

    starts = (jnp.asarray(sp_order, jnp.int32) ^ me) * local_len
    pos = (starts[:, None] + jnp.arange(local_len, dtype=jnp.int32)).reshape(-1)
    lane = jnp.arange(LANES, dtype=jnp.int32) % (ROT // 2)
    freq = 1.0 / 10000.0 ** ((2 * lane).astype(F32) / ROT)
    angles = pos.astype(F32)[:, None] * freq[None, :]
    joined_row = jnp.pad(joined_add, (0, wide - cols))[None]
    ap, ea, joined_g, dense_g, a_sums, j_sums = attention(
        ids,
        xs,
        cots,
        joined_w,
        dense_w,
        stacked([whole(4), whole(5)]),
        joined_row,
        (jnp.cos(angles), jnp.sin(angles)),
        (pos[:, None], pos[None, :]),
        seqs,
        heads,
    )
    dense_g = dense_g.reshape(dp // sp, sp, row_n, width).transpose(1, 0, 2, 3)
    dense_g = dense_g.reshape(heads * HD, width)
    dense_g = lax.all_to_all(dense_g, "sp", split_axis=0, concat_axis=0, tiled=True)
    dense_g = jnp.pad(dense_g.reshape(dp, row_n, width), ((0, 0), (0, -row_n % 8), (0, 0)))
    expand_g, shrink_g, keep, send, m_sums = feed_forward(
        ids,
        xs,
        cots,
        expand_w,
        shrink_w,
        ap,
        ea,
        stacked([whole(6), whole(7), expand_add]),
        dense_g,
    )

    got = swap(send, "sp", 1)
    parts = keep.astype(F32) + got.astype(F32)
    for bit in bits_of(sp)[1:]:
        half = parts.shape[0] // 2
        got = swap(parts[half:].astype(BF), "sp", bit)
        parts = parts[:half] + got.astype(F32)
    out_sum, scaled = parts[0, 0], parts[0, 1]
    rows = inputs.reshape(local, width).astype(F32)
    output = (rows + out_sum + out_add).astype(BF).reshape(inputs.shape)
    own_normed, own_inv = layer_norm(rows)
    first = jnp.mean(scaled, axis=-1, keepdims=True)
    second = jnp.mean(scaled * own_normed, axis=-1, keepdims=True)
    cot_f = cotangent.reshape(local, width).astype(F32)
    input_grad = cot_f + own_inv * (scaled - first - own_normed * second)
    input_grad = input_grad.reshape(inputs.shape)

    joined_b_all = lax.dynamic_update_slice_in_dim(
        jnp.zeros((cols * sp,), F32), j_sums[0, :cols], me * cols, 0
    )
    mine = (jnp.arange(sp, dtype=jnp.int32) == me)[None, :, None]
    expand_b_all = jnp.where(mine, m_sums[0, :units].reshape(dp, 1, ff_n), 0.0)

    def split(vector):
        vector = vector.reshape(dp, sp, -1)
        return jnp.pad(vector, ((0, 0), (0, 0), (0, LANES - vector.shape[2])))

    vectors = [joined_b_all, expand_b_all, jnp.sum(cot_f, axis=0)]
    vectors += [a_sums[0], a_sums[1], m_sums[1], m_sums[2]]
    small_g = jnp.stack([split(v) for v in vectors] + [jnp.zeros((dp, sp, LANES), F32)], axis=1)
    small_g = turn_bits(flip_bits(small_g, "dp")).reshape(dp, 8, sp * LANES)
    small_g = jnp.pad(small_g, ((0, 0), (0, 0), (0, width - sp * LANES))).astype(BF)
    small_at = shrink_g.shape[1] - 8
    shrink_g = lax.dynamic_update_slice(shrink_g, small_g, (0, small_at, 0))

    joined_g = cube_scatter(joined_g, "dp", BF)[0, :, :cols].astype(BF)
    joined_g = lax.all_to_all(joined_g, "sp", split_axis=0, concat_axis=1, tiled=True)
    expand_g = cube_scatter(expand_g, "dp", BF)[0].astype(BF)
    expand_g = lax.all_to_all(expand_g, "sp", split_axis=0, concat_axis=1, tiled=True)
    expand_g = expand_g.reshape(row_n, sp, dp, ff_n).transpose(0, 2, 1, 3).reshape(row_n, -1)
    shrink_g = cube_scatter(shrink_g, "dp", BF)[0]
    small_g = shrink_g[small_at:, : sp * LANES].reshape(8, sp, LANES).transpose(1, 0, 2)
    small_g = cube_scatter(turn_bits(flip_bits(small_g, "sp")), "sp", F32)[0]
    names = [0, 2, 1, 4, 5, 6, 7]
    pieces = [small_g[i, : sizes[name]] for i, name in enumerate(names)]
    joined_bg, expand_bg, out_bg, gain_ag, shift_ag, gain_bg, shift_bg = pieces
    return (
        output,
        input_grad,
        joined_g.astype(F32),
        joined_bg,
        shrink_g[ff_n : ff_n + row_n],
        out_bg,
        expand_g.astype(F32),
        expand_bg,
        shrink_g[:ff_n],
        out_bg,
        gain_ag,
        shift_ag,
        gain_bg,
        shift_bg,
    )


def solution(mesh):
    token = P("dp", "sp", None)
    matrix = P(("dp", "sp"), None)
    vector = P(("dp", "sp"))
    params = (matrix, vector) * 4 + (vector,) * 4
    return jax.shard_map(
        on_device,
        mesh=mesh,
        in_specs=(token, token) + params,
        out_specs=(token, token) + params,
        check_vma=False,
    )
```

```python
import functools

import jax
import jax.numpy as jnp
from jax import lax
from jax.experimental import pallas as pl
from jax.experimental.pallas import tpu as pltpu
from jax.sharding import PartitionSpec as P


HEADS = 12
HD = 64
ROT = 16
LANES = 128
NORM_EPS = 1e-05
BF = jnp.bfloat16
F32 = jnp.float32
VMEM_LIMIT = 60 * 1024 * 1024


def bits_of(count):
    assert count & (count - 1) == 0
    bit = 1
    out = []
    while bit < count:
        out.append(bit)
        bit *= 2
    return out


def cube_order(count):
    order = [0]
    for bit in reversed(bits_of(count)):
        order = order + [k ^ bit for k in order]
    return order


def swap(value, axis, bit):
    count = lax.axis_size(axis)
    return lax.ppermute(value, axis, [(i, i ^ bit) for i in range(count)])


def halves(block, axis):
    mine, got = None, block[None]
    for bit in reversed(bits_of(lax.axis_size(axis))):
        mine = got if mine is None else jnp.concatenate([mine, got], axis=0)
        got = swap(mine, axis, bit)
    return mine, got


def token_blocks(block, axis):
    blocks = [block]
    for bit in reversed(bits_of(lax.axis_size(axis))):
        more = []
        for b in blocks:
            more.append(swap(b, axis, bit))
        blocks = blocks + more
    return blocks


def transposed(value, back):
    dp, sp = lax.axis_size("dp"), lax.axis_size("sp")
    perm = [(s * dp + b, b * sp + s) for s in range(sp) for b in range(dp)]
    if back:
        perm = [(to, at) for at, to in perm]
    return lax.ppermute(value, ("dp", "sp"), perm)


def cube_scatter(keep, send, axis):
    for bit in bits_of(lax.axis_size(axis)):
        got = swap(send, axis, bit)
        half = keep.shape[0] // 2
        if half:
            send = (keep[half:].astype(F32) + got[half:].astype(F32)).astype(BF)
            keep = keep[:half].astype(F32) + got[:half].astype(F32)
    return keep[0], got[0]


def flip_bits(blocks, axis):
    count = lax.axis_size(axis)
    me = lax.axis_index(axis)
    rest = blocks.shape[1:]
    for bit in bits_of(count):
        pairs = blocks.reshape((count // (2 * bit), 2, bit) + rest)
        blocks = jnp.where((me & bit) > 0, pairs[:, ::-1], pairs).reshape((count,) + rest)
    return blocks


def turn_bits(blocks):
    count = blocks.shape[0]
    bits = len(bits_of(count))
    rest = blocks.shape[1:]
    blocks = blocks.reshape((2,) * bits + rest)
    axes = tuple(reversed(range(bits))) + tuple(range(bits, bits + len(rest)))
    return blocks.transpose(axes).reshape((count,) + rest)


def layer_norm(values):
    mean_val = jnp.mean(values, axis=-1, keepdims=True)
    centred = values - mean_val
    variance = jnp.mean(centred * centred, axis=-1, keepdims=True)
    inv_std = lax.rsqrt(variance + NORM_EPS)
    return centred * inv_std, inv_std


def dot(left, right, left_dim, right_dim):
    dims = (((left_dim,), (right_dim,)), ((), ()))
    return lax.dot_general(left, right, dims, preferred_element_type=F32)


def row_sum(value):
    return jnp.sum(value, axis=0, keepdims=True)


def copies_in(blocks, target, rows, sem):
    out = []
    for i, block in enumerate(blocks):
        out.append(pltpu.make_async_copy(block, target.at[pl.ds(i * rows, rows)], sem.at[i]))
    return out


def placed(ids, mine, got, target, rows, width, sem):
    out = []
    half = mine.shape[0]
    for p in range(2 * half):
        source = mine.at[p] if p < half else got.at[p - half]
        if source.shape != (rows, width):
            source = source.at[pl.ds(0, rows), pl.ds(0, width)]
        to = pl.multiple_of(ids[p] * rows, 8)
        out.append(pltpu.make_async_copy(source, target.at[pl.ds(to, rows)], sem.at[p]))
    return out


def sent(ids, source, keep, send, rows, sem):
    todo = []
    half = keep.shape[0]
    for p in range(2 * half):
        at = pl.multiple_of(ids[p] * rows, 8)
        to = keep.at[p] if p < half else send.at[p - half]
        if to.shape[0] != rows:
            to = to.at[pl.ds(0, rows)]
        todo.append(pltpu.make_async_copy(source.at[pl.ds(at, rows)], to, sem.at[p]))
    return todo


def run(copies):
    for copy in copies:
        copy.start()


def finish(copies):
    for copy in copies:
        copy.wait()


def grad_rows(left, right, out):
    rows = 256

    @pl.loop(0, left.shape[1] // rows)
    def _(r):
        at = pl.ds(pl.multiple_of(r * rows, rows), rows)
        out[at, : right.shape[1]] = dot(left[:, at], right[...], 0, 0).astype(BF)


def mlp_kernel(sp, ids, *refs):
    xs, cots = refs[:sp], refs[sp : 2 * sp]
    ew_mine, ew_got, sw_mine, sw_got, vec = refs[2 * sp : 2 * sp + 5]
    outs = refs[2 * sp + 5 : 2 * sp + 12]
    eg_keep, eg_send, sg_keep, sg_send, out_part, in_part, sums = outs
    x, cot, ew, sw, hid, act, pgr, eg, sg, sem = refs[2 * sp + 12 :]
    width = x.shape[1]
    chunk = x.shape[0] // sp
    rows, units = eg_keep.shape[1], sg_keep.shape[1]
    gets = (
        copies_in([b.at[pl.ds(0, chunk)] for b in xs], x, chunk, sem.at[0])
        + copies_in([b.at[pl.ds(0, chunk)] for b in cots], cot, chunk, sem.at[1])
        + placed(ids, ew_mine, ew_got, ew, rows, ew.shape[1], sem.at[2])
        + placed(ids, sw_mine, sw_got, sw, units, width, sem.at[3])
    )
    run(gets)
    sums[...] = jnp.zeros_like(sums)
    finish(gets)
    gain, shift, add = vec[0:1, :], vec[1:2, :], vec[2:3, : ew.shape[1]]

    @pl.loop(0, sp)
    def _(k):
        at = pl.ds(pl.multiple_of(k * chunk, chunk), chunk)
        normed, _ = layer_norm(x[at, :].astype(F32))
        hidden = (normed * gain + shift).astype(BF)
        hid[at, :] = hidden
        pre = dot(hidden, ew[...], 1, 0) + add
        cdf = 0.5 * (1.0 + lax.erf(pre * 0.7071067811865476))
        activated = (pre * cdf).astype(BF)
        act[at, :] = activated
        slope = cdf + pre * jnp.exp(-0.5 * pre * pre) * 0.3989422804014327
        pre_grad = dot(cot[at, :], sw[...], 1, 1) * slope
        sums[0:1, : ew.shape[1]] += row_sum(pre_grad)
        pre_grad_bf = pre_grad.astype(BF)
        pgr[at, :] = pre_grad_bf
        out_part[k] = dot(activated, sw[...], 1, 0).astype(BF)
        hidden_grad = dot(pre_grad_bf, ew[...], 1, 1)
        sums[1:2, :] += row_sum(hidden_grad * normed)
        sums[2:3, :] += row_sum(hidden_grad)
        in_part[k] = (hidden_grad * gain).astype(BF)

    grad_rows(hid, pgr, eg)
    puts = sent(ids, eg, eg_keep, eg_send, rows, sem.at[0])
    run(puts)
    grad_rows(act, cot, sg)
    more = sent(ids, sg, sg_keep, sg_send, units, sem.at[1])
    run(more)
    finish(puts + more)


def attn_kernel(sp, seqs, heads, ids, *refs):
    xs, cots = refs[:sp], refs[sp : 2 * sp]
    jw_mine, jw_got, dw, vec, jadd, cos_ref, sin_ref, posc, posr = refs[2 * sp : 2 * sp + 9]
    out_part, in_part, m_sums, g_keep, g_send, keep, send = refs[2 * sp + 9 : 2 * sp + 16]
    x, cot, jw, hid, rot, cg, ctx, jgf, jgb, ctk, gr, sums, small, sem = refs[2 * sp + 16 :]
    width = x.shape[1]
    wide = jw.shape[1]
    cols = heads * 3 * HD
    chunk = x.shape[0] // sp
    part = chunk // seqs
    full = part * sp
    half = g_keep.shape[0]
    rows = width // (2 * half)
    per = rows // sp
    scale = HD ** (-0.5)
    gets = (
        copies_in([b.at[pl.ds(0, chunk)] for b in xs], x, chunk, sem.at[0])
        + copies_in([b.at[pl.ds(0, chunk)] for b in cots], cot, chunk, sem.at[1])
        + placed(ids, jw_mine, jw_got, jw, rows, wide, sem.at[2])
    )
    run(gets)
    sums[...] = jnp.zeros_like(sums)
    jgf[:, cols:] = jnp.zeros((jgf.shape[0], wide - cols), F32)
    finish(gets)
    gain, shift = vec[0:1, :], vec[1:2, :]

    def tables(g, k):
        at = pl.ds(pl.multiple_of(k * part, part), part)
        lane = lax.broadcasted_iota(jnp.int32, (part, LANES), 1)
        col = lane + g * LANES
        inner = col % HD
        turned = (inner < ROT) & ((col // HD) % 3 < 2) & (col < cols)
        cos_val, sin_val = cos_ref[at, :], sin_ref[at, :]
        low = jnp.where(turned & (inner < ROT // 2), sin_val, 0.0)
        high = jnp.where(turned & (inner >= ROT // 2), sin_val, 0.0)
        both = [jnp.where(turned, cos_val, 1.0), low, high]
        return [jnp.concatenate([t] * seqs, axis=0) for t in both]

    def rotate(value, g, k, sign):
        cos_val, low, high = tables(g, k)
        up = pltpu.roll(value, LANES - ROT // 2, 1)
        down = pltpu.roll(value, ROT // 2, 1)
        return value * cos_val + sign * (down * high - up * low)

    def spread(ref, k, lanes, value):
        for b in range(seqs):
            at = pl.ds(pl.multiple_of(b * full + k * part, part), part)
            ref[at, lanes] = value[b * part : (b + 1) * part]

    def collect(ref, k, lanes):
        at = [pl.ds(pl.multiple_of(b * full + k * part, part), part) for b in range(seqs)]
        return jnp.concatenate([ref[a, lanes] for a in at], axis=0)

    @pl.loop(0, sp)
    def _(k):
        at = pl.ds(pl.multiple_of(k * chunk, chunk), chunk)
        normed, _ = layer_norm(x[at, :].astype(F32))
        hidden = (normed * gain + shift).astype(BF)
        hid[at, :] = hidden
        joined = dot(hidden, jw[...], 1, 0) + jadd[...]
        for g in range(wide // LANES):
            lanes = slice(g * LANES, (g + 1) * LANES)
            spread(rot, k, lanes, rotate(joined[:, lanes], g, k, 1.0).astype(BF))
        spread(cg, k, slice(None), dot(cot[at, :], dw[...], 1, 1).astype(BF))

    allowed = posc[...] >= posr[...]

    @pl.loop(0, seqs)
    def _(b):
        at = pl.ds(pl.multiple_of(b * full, full), full)
        for h in range(heads):
            q0 = h * 3 * HD
            query = rot[at, q0 : q0 + HD]
            key = rot[at, q0 + HD : q0 + 2 * HD]
            value = rot[at, q0 + 2 * HD : q0 + 3 * HD]
            grad = cg[at, h * HD : (h + 1) * HD]
            scores = dot(query, key, 1, 1) * scale
            total = jnp.sum(jnp.where(allowed, jnp.exp(scores), 0.0), axis=-1, keepdims=True)
            probs = jnp.where(allowed, jnp.exp(scores - jnp.log(total)), 0.0)
            weights = probs.astype(BF)
            context = dot(weights, value, 1, 0)
            ctx[at, h * HD : (h + 1) * HD] = context.astype(BF)
            delta = jnp.sum(grad.astype(F32) * context, axis=-1, keepdims=True)
            jgf[at, q0 + 2 * HD : q0 + 3 * HD] = dot(weights, grad, 0, 0)
            score_grad = (probs * (dot(grad, value, 1, 1) - delta) * scale).astype(BF)
            jgf[at, q0 : q0 + HD] = dot(score_grad, key, 1, 0)
            jgf[at, q0 + HD : q0 + 2 * HD] = dot(score_grad, query, 0, 0)

    @pl.loop(0, sp)
    def _(k):
        at = pl.ds(pl.multiple_of(k * chunk, chunk), chunk)
        for g in range(wide // LANES):
            lanes = slice(g * LANES, (g + 1) * LANES)
            back = rotate(collect(jgf, k, lanes), g, k, -1.0).astype(BF)
            jgb[at, lanes] = back
            sums[5:6, lanes] += row_sum(back.astype(F32))
        hidden_grad = dot(jgb[at, :], jw[...], 1, 1)
        normed, _ = layer_norm(x[at, :].astype(F32))
        sums[0:1, :] += row_sum(hidden_grad * normed)
        sums[1:2, :] += row_sum(hidden_grad)
        context = collect(ctx, k, slice(None))
        ctk[at, :] = context
        scaled = (hidden_grad * gain + in_part[k].astype(F32)).astype(BF)
        out_sum = (dot(context, dw[...], 1, 0) + out_part[k].astype(F32)).astype(BF)

        @pl.when(k < sp // 2)
        def _():
            keep[k, 0] = out_sum
            keep[k, 1] = scaled

        @pl.when(k >= sp // 2)
        def _():
            send[k - sp // 2, 0] = out_sum
            send[k - sp // 2, 1] = scaled

    sums[2:4, :] = m_sums[1:3, :]
    sums[4:5, :] = row_sum(cot[0:chunk, :].astype(F32))
    sums[6:7, :] = m_sums[0:1, :]
    small[...] = sums[...].astype(BF)
    puts = []
    for p in range(2 * half):
        to = g_keep.at[p] if p < half else g_send.at[p - half]
        puts.append(pltpu.make_async_copy(small, to.at[pl.ds(rows, 8)], sem.at[1, p]))
    run(puts)
    grad_rows(hid, jgb, gr)
    dense_g = dot(ctk[...], cot[...], 0, 0).astype(BF)
    lanes = width - cols
    for d in range(2 * half):
        for q in range(sp):
            piece = dense_g[d * per : (d + 1) * per, q * lanes : (q + 1) * lanes]
            gr[d * rows + q * per : d * rows + (q + 1) * per, cols:] = piece
    more = sent(ids, gr, g_keep, g_send, rows, sem.at[0])
    run(more)
    finish(puts + more)


ANY = pl.BlockSpec(memory_space=pl.ANY)
IN_VMEM = pl.BlockSpec(memory_space=pltpu.VMEM)
IN_SMEM = pl.BlockSpec(memory_space=pltpu.SMEM)


def call(body, args, specs, outs, out_specs, scratch, flops):
    moved = sum(a.size * a.dtype.itemsize for a in args)
    moved += sum(o.size * o.dtype.itemsize for o in outs)
    return pl.pallas_call(
        body,
        in_specs=specs,
        out_shape=outs,
        out_specs=out_specs,
        scratch_shapes=scratch,
        compiler_params=pltpu.CompilerParams(vmem_limit_bytes=VMEM_LIMIT),
        cost_estimate=pl.CostEstimate(flops=flops, bytes_accessed=moved, transcendentals=0),
    )(*args)


def tidy(body, args, outs):
    specs = [IN_SMEM if a.dtype == jnp.int32 else IN_VMEM for a in args]
    return call(body, args, specs, outs, [IN_VMEM] * len(outs), [], 0)


def split_weights(sp, dp, expand, joined, out):
    rows = expand.shape[0]
    each = expand.shape[1] // (sp * dp)
    cols = joined.shape[1] // sp
    for s in range(sp):
        for d in range(dp):
            at = (d * sp + s) * each
            out[s, :rows, d * each : (d + 1) * each] = expand[:, at : at + each]
        out[s, rows:, :cols] = joined[:, s * cols : (s + 1) * cols]
        out[s, rows:, cols:] = jnp.zeros((rows, out.shape[2] - cols), out.dtype)


def split_grads(sp, cols, keep, got, last, dense):
    value = (keep[...] + got[...].astype(F32)).astype(BF)
    rows = value.shape[0] - 8
    per = rows // sp
    lanes = value.shape[1] - cols
    for s in range(sp):
        last[s, :per] = value[s * per : (s + 1) * per]
        last[s, per:] = value[rows:]
        dense[:, s * lanes : (s + 1) * lanes] = value[s * per : (s + 1) * per, cols:]


def join_grads(sp, cols, at, last, out, small):
    per = out.shape[0]
    width = last.shape[2]
    total = jnp.zeros((8, width), F32)
    joined = jnp.zeros((8, width), F32)
    for s in range(sp):
        out[:, s * cols : (s + 1) * cols] = last[s, :per, :cols].astype(F32)
        block = last[s, per:].astype(F32)
        total = total + block
        joined = joined + jnp.where(at[0] == s, block, 0.0)
    row = lax.broadcasted_iota(jnp.int32, (8, LANES), 0)
    mine = last[at[4], per:].astype(F32)
    sums = pltpu.roll(total, at[1], 1)[:, :LANES]
    joined = pltpu.roll(joined, at[2], 1)[:, :LANES]
    mine = pltpu.roll(mine, at[3], 1)[:, :LANES]
    small[...] = jnp.where(row < 5, sums, jnp.where(row == 5, joined, mine))


def join_expand(sp, dp, parts, out):
    each = parts.shape[2] // dp
    for s in range(sp):
        for d in range(dp):
            at = (d * sp + s) * each
            out[:, at : at + each] = parts[s, :, d * each : (d + 1) * each].astype(F32)


def finish_tokens(x, cot, keep, got, add, out, grad):
    rows = x[...].astype(F32)
    sums = keep[...].astype(F32) + got[...].astype(F32)
    out[...] = (rows + sums[0] + add[...]).astype(BF)
    scaled = sums[1]
    normed, inv = layer_norm(rows)
    first = jnp.mean(scaled, axis=-1, keepdims=True)
    second = jnp.mean(scaled * normed, axis=-1, keepdims=True)
    grad[...] = cot[...].astype(F32) + inv * (scaled - first - normed * second)


def attention(ids, xs, cots, jw, dw, vec, jadd, tables, poss, parts, seqs, heads):
    sp = len(xs)
    chunk, width = parts[0].shape[1:]
    tokens = sp * chunk
    wide = jadd.shape[1]
    dp = 2 * jw[0].shape[0]
    rows = width // dp
    shape = jax.ShapeDtypeStruct
    outs = [
        shape((dp // 2, rows + 8, width), BF),
        shape((dp // 2, rows + 8, width), BF),
        shape((sp // 2, 2, chunk, width), BF),
        shape((sp // 2, 2, chunk, width), BF),
    ]
    scratch = [
        pltpu.VMEM((tokens, width), BF),
        pltpu.VMEM((tokens, width), BF),
        pltpu.VMEM((width, wide), BF),
        pltpu.VMEM((tokens, width), BF),
        pltpu.VMEM((tokens, wide), BF),
        pltpu.VMEM((tokens, heads * HD), BF),
        pltpu.VMEM((tokens, heads * HD), BF),
        pltpu.VMEM((tokens, wide), F32),
        pltpu.VMEM((tokens, wide), BF),
        pltpu.VMEM((tokens, heads * HD), BF),
        pltpu.VMEM((width, width), BF),
        pltpu.VMEM((8, width), F32),
        pltpu.VMEM((8, width), BF),
        pltpu.SemaphoreType.DMA((3, max(dp, sp))),
    ]
    return call(
        functools.partial(attn_kernel, sp, seqs, heads),
        [ids, *xs, *cots, *jw, dw, vec, jadd, *tables, *poss, *parts],
        [IN_SMEM] + [ANY] * (2 * sp + 2) + [IN_VMEM] * 10,
        outs,
        [ANY, ANY, IN_VMEM, IN_VMEM],
        scratch,
        24 * tokens * width * wide,
    )


def feed_forward(ids, xs, cots, ew, sw, vec, chunk):
    sp = len(xs)
    width = xs[0].shape[1]
    tokens = sp * chunk
    units = ew[0].shape[2]
    dp = 2 * ew[0].shape[0]
    rows, per = width // dp, sw[0].shape[1]
    shape = jax.ShapeDtypeStruct
    outs = [
        shape((dp // 2, rows, units), BF),
        shape((dp // 2, rows, units), BF),
        shape((dp // 2, per, width), BF),
        shape((dp // 2, per, width), BF),
        shape((sp, chunk, width), BF),
        shape((sp, chunk, width), BF),
        shape((8, width), F32),
    ]
    scratch = [
        pltpu.VMEM((tokens, width), BF),
        pltpu.VMEM((tokens, width), BF),
        pltpu.VMEM((width, units), BF),
        pltpu.VMEM((units, width), BF),
        pltpu.VMEM((tokens, width), BF),
        pltpu.VMEM((tokens, units), BF),
        pltpu.VMEM((tokens, units), BF),
        pltpu.VMEM((width, units), BF),
        pltpu.VMEM((units, width), BF),
        pltpu.SemaphoreType.DMA((4, max(dp, sp))),
    ]
    return call(
        functools.partial(mlp_kernel, sp),
        [ids, *xs, *cots, *ew, *sw, vec],
        [IN_SMEM] + [ANY] * (2 * sp + 4) + [IN_VMEM],
        outs,
        [ANY, ANY, ANY, ANY, IN_VMEM, IN_VMEM, IN_VMEM],
        scratch,
        20 * tokens * width * units,
    )


def on_device(
    inputs,
    cotangent,
    joined_weight,
    joined_bias,
    dense_weight,
    dense_bias,
    expand_weight,
    expand_bias,
    shrink_weight,
    shrink_bias,
    attn_gain,
    attn_shift,
    mlp_gain,
    mlp_shift,
):
    seqs, local_len, width = inputs.shape
    sp, dp = lax.axis_size("sp"), lax.axis_size("dp")
    me, dp_me = lax.axis_index("sp"), lax.axis_index("dp")
    heads = HEADS // sp
    local = seqs * local_len
    cols = joined_weight.shape[1] // sp
    wide = -(-cols // LANES) * LANES
    row_n = joined_weight.shape[0]
    rows_d = row_n * sp
    ff_n = shrink_weight.shape[0]
    units = ff_n * dp
    sp_order, dp_order = cube_order(sp), cube_order(dp)
    ids = jnp.asarray(dp_order, jnp.int32) ^ dp_me

    shape = jax.ShapeDtypeStruct
    split = functools.partial(split_weights, sp, dp)
    outs = [shape((sp, 2 * row_n, units), BF)]
    (both,) = tidy(split, [expand_weight, joined_weight], outs)
    both = lax.all_to_all(both, "sp", split_axis=0, concat_axis=0, tiled=True)
    expand_part = both[:, :row_n].reshape(rows_d, units)
    joined_part = both[:, row_n:, :wide].reshape(rows_d, wide)

    small_parts = (
        joined_bias,
        dense_bias,
        expand_bias,
        shrink_bias,
        attn_gain,
        attn_shift,
        mlp_gain,
        mlp_shift,
    )
    sizes = [part.shape[0] for part in small_parts]
    row = jnp.arange(8, dtype=jnp.int32)[:, None]
    small = jnp.zeros((8, width), BF)
    for i, part in enumerate(small_parts):
        small = jnp.where(row == i, jnp.pad(part, (0, width - part.shape[0]))[None], small)
    xs = token_blocks(inputs.reshape(local, width), "sp")
    cots = token_blocks(jnp.concatenate([cotangent.reshape(local, width), small]), "sp")
    small = jnp.stack([block[local:, :LANES] for block in cots])
    small = flip_bits(turn_bits(small), "sp").transpose(1, 0, 2).reshape(8, sp * LANES)
    small = halves(small, "dp")
    small = flip_bits(turn_bits(jnp.concatenate(small, axis=0)), "dp")
    small = small.reshape(dp, 8, sp, LANES).astype(F32)

    dense_part = transposed(dense_weight, False)
    shrink_w = halves(shrink_weight, "dp")
    expand_w = halves(jnp.concatenate([expand_part, dense_part]), "dp")
    joined_w = halves(joined_part, "dp")

    dense_w = jnp.concatenate([half[:, rows_d:] for half in expand_w], axis=0)
    dense_w = flip_bits(turn_bits(dense_w), "dp").reshape(heads * HD, width)

    def whole(index):
        return small[:, index, :, : sizes[index]].reshape(-1)

    joined_add = lax.dynamic_slice_in_dim(whole(0), me * cols, cols)
    out_add = whole(1) + whole(3)
    expand_add = lax.dynamic_index_in_dim(small[:, 2], me, 1, keepdims=False)[:, : sizes[2]]

    def stacked(vectors):
        vectors = [jnp.pad(v.reshape(-1), (0, width - v.size)) for v in vectors]
        return jnp.stack(vectors + [jnp.zeros((width,), F32)] * (8 - len(vectors)))

    starts = (jnp.asarray(sp_order, jnp.int32) ^ me) * local_len
    pos = (starts[:, None] + jnp.arange(local_len, dtype=jnp.int32)).reshape(-1)
    lane = jnp.arange(LANES, dtype=jnp.int32) % (ROT // 2)
    freq = 1.0 / 10000.0 ** ((2 * lane).astype(F32) / ROT)
    angles = pos.astype(F32)[:, None] * freq[None, :]
    joined_row = jnp.pad(joined_add, (0, wide - cols))[None]
    e_keep, e_send, s_keep, s_send, *parts = feed_forward(
        ids,
        xs,
        cots,
        expand_w,
        shrink_w,
        stacked([whole(6), whole(7), expand_add]),
        local,
    )
    a_keep, a_send, keep, send = attention(
        ids,
        xs,
        cots,
        joined_w,
        dense_w,
        stacked([whole(4), whole(5)]),
        joined_row,
        (jnp.cos(angles), jnp.sin(angles)),
        (pos[:, None], pos[None, :]),
        parts,
        seqs,
        heads,
    )

    keep, got = cube_scatter(keep, send, "sp")
    output, input_grad = tidy(
        finish_tokens,
        [
            inputs.reshape(local, width),
            cotangent.reshape(local, width),
            keep,
            got,
            out_add[None],
        ],
        [shape((local, width), BF), shape((local, width), F32)],
    )
    output, input_grad = output.reshape(inputs.shape), input_grad.reshape(inputs.shape)

    keep, got = cube_scatter(s_keep, s_send, "dp")
    shrink_g = keep + got.astype(F32)
    keep, got = cube_scatter(e_keep, e_send, "dp")
    expand_g = (keep + got.astype(F32)).astype(BF).reshape(sp, row_n, units)
    expand_g = lax.all_to_all(expand_g, "sp", split_axis=0, concat_axis=0, tiled=True)
    (expand_g,) = tidy(
        functools.partial(join_expand, sp, dp), [expand_g], [shape(expand_weight.shape, F32)]
    )
    keep, got = cube_scatter(a_keep, a_send, "dp")
    last, dense_g = tidy(
        functools.partial(split_grads, sp, cols),
        [keep, got],
        [shape((sp, row_n + 8, width), BF), shape((row_n, width), BF)],
    )
    last = lax.all_to_all(last, "sp", split_axis=0, concat_axis=0, tiled=True)
    dense_g = transposed(dense_g, True)
    own_b = joined_bias.shape[0]
    linear = dp_me * sp + me
    holder = linear * own_b // cols
    starts = [linear * row_n, linear * own_b - holder * cols, dp_me * ff_n]
    at = [holder] + [(width - start) % width for start in starts] + [me]
    joined_g, small_g = tidy(
        functools.partial(join_grads, sp, cols),
        [jnp.stack(at).astype(jnp.int32), last],
        [shape(joined_weight.shape, F32), shape((8, LANES), F32)],
    )
    joined_bg, expand_bg = small_g[5, :own_b], small_g[6, :ff_n]
    gain_ag, shift_ag, gain_bg, shift_bg, out_bg = [small_g[i, :row_n] for i in range(5)]
    return (
        output,
        input_grad,
        joined_g,
        joined_bg,
        dense_g.astype(F32),
        out_bg,
        expand_g,
        expand_bg,
        shrink_g,
        out_bg,
        gain_ag,
        shift_ag,
        gain_bg,
        shift_bg,
    )


def solution(mesh):
    token = P("dp", "sp", None)
    matrix = P(("dp", "sp"), None)
    vector = P(("dp", "sp"))
    params = (matrix, vector) * 4 + (vector,) * 4
    return jax.shard_map(
        on_device,
        mesh=mesh,
        in_specs=(token, token) + params,
        out_specs=(token, token) + params,
        check_vma=False,
    )
```

```python
import functools

import jax
import jax.numpy as jnp
from jax import lax
from jax.experimental import pallas as pl
from jax.experimental.pallas import tpu as pltpu
from jax.sharding import PartitionSpec as P


HEADS = 12
HD = 64
ROT = 16
LANES = 128
SPLITS = 2
NORM_EPS = 1e-05
BF = jnp.bfloat16
F32 = jnp.float32
VMEM_LIMIT = 60 * 1024 * 1024


def bits_of(count):
    assert count & (count - 1) == 0
    bit = 1
    out = []
    while bit < count:
        out.append(bit)
        bit *= 2
    return out


def cube_order(bits):
    order = [0]
    for bit in reversed(bits):
        order = order + [k ^ bit for k in order]
    return order


def side_first(count):
    bits = bits_of(count)
    return [bits[1], bits[0], *bits[2:]]


def swap(value, axis, bit):
    count = lax.axis_size(axis)
    return lax.ppermute(value, axis, [(i, i ^ bit) for i in range(count)])


def halves(block, axis, bits):
    mine, got = None, block[None]
    for bit in reversed(bits):
        mine = got if mine is None else jnp.concatenate([mine, got], axis=0)
        got = swap(mine, axis, bit)
    return mine, got


def token_blocks(block, axis):
    blocks = [block]
    for bit in reversed(bits_of(lax.axis_size(axis))):
        more = []
        for b in blocks:
            more.append(swap(b, axis, bit))
        blocks = blocks + more
    return blocks


def transposed(value, back):
    dp, sp = lax.axis_size("dp"), lax.axis_size("sp")
    perm = [(s * dp + b, b * sp + s) for s in range(sp) for b in range(dp)]
    if back:
        perm = [(to, at) for at, to in perm]
    return lax.ppermute(value, ("dp", "sp"), perm)


def cube_scatter(keep, send, axis, bits):
    for bit in bits:
        got = swap(send, axis, bit)
        half = keep.shape[0] // 2
        if half:
            send = (keep[half:].astype(F32) + got[half:].astype(F32)).astype(BF)
            keep = keep[:half].astype(F32) + got[:half].astype(F32)
    return keep[0], got[0]


def flip_bits(blocks, axis):
    count = lax.axis_size(axis)
    me = lax.axis_index(axis)
    rest = blocks.shape[1:]
    for bit in bits_of(count):
        pairs = blocks.reshape((count // (2 * bit), 2, bit) + rest)
        blocks = jnp.where((me & bit) > 0, pairs[:, ::-1], pairs).reshape((count,) + rest)
    return blocks


def turn_bits(blocks):
    count = blocks.shape[0]
    bits = len(bits_of(count))
    rest = blocks.shape[1:]
    blocks = blocks.reshape((2,) * bits + rest)
    axes = tuple(reversed(range(bits))) + tuple(range(bits, bits + len(rest)))
    return blocks.transpose(axes).reshape((count,) + rest)


def layer_norm(values):
    mean_val = jnp.mean(values, axis=-1, keepdims=True)
    centred = values - mean_val
    variance = jnp.mean(centred * centred, axis=-1, keepdims=True)
    inv_std = lax.rsqrt(variance + NORM_EPS)
    return centred * inv_std, inv_std


def dot(left, right, left_dim, right_dim):
    dims = (((left_dim,), (right_dim,)), ((), ()))
    return lax.dot_general(left, right, dims, preferred_element_type=F32)


def row_sum(value):
    return jnp.sum(value, axis=0, keepdims=True)


def copies_in(blocks, target, rows, sem):
    out = []
    for i, block in enumerate(blocks):
        out.append(pltpu.make_async_copy(block, target.at[pl.ds(i * rows, rows)], sem.at[i]))
    return out


def placed(ids, mine, got, target, rows, width, sem, first=0):
    out = []
    half = mine.shape[0]
    for p in range(2 * half):
        source = mine.at[p] if p < half else got.at[p - half]
        if source.shape != (rows, width):
            source = source.at[pl.ds(0, rows), pl.ds(0, width)]
        to = pl.multiple_of(ids[first + p] * rows, 8)
        out.append(pltpu.make_async_copy(source, target.at[pl.ds(to, rows)], sem.at[p]))
    return out


def sent(ids, source, keep, send, rows, sem, first=0):
    todo = []
    half = keep.shape[0]
    for p in range(2 * half):
        at = pl.multiple_of(ids[first + p] * rows, 8)
        to = keep.at[p] if p < half else send.at[p - half]
        if to.shape[0] != rows:
            to = to.at[pl.ds(0, rows)]
        todo.append(pltpu.make_async_copy(source.at[pl.ds(at, rows)], to, sem.at[p]))
    return todo


def run(copies):
    for copy in copies:
        copy.start()


def finish(copies):
    for copy in copies:
        copy.wait()


def grad_rows(left, right, out):
    rows = 256

    @pl.loop(0, left.shape[1] // rows)
    def _(r):
        at = pl.ds(pl.multiple_of(r * rows, rows), rows)
        out[at, : right.shape[1]] = dot(left[:, at], right[...], 0, 0).astype(BF)


def unpack(sp, me, small, row_n, own_b, vecs, eadd, jadd):
    dp = small.shape[0]
    ff_n = eadd.shape[1] // dp
    for d in range(dp):
        block = small[d].astype(F32)
        for s in range(sp):
            at = (d * sp + s) * row_n
            vecs[:, at : at + row_n] = block[:, s * LANES : s * LANES + row_n]
        lanes = pl.ds(pl.multiple_of(me * LANES, LANES), LANES)
        mine = small[d, :, lanes].astype(F32)
        eadd[:, d * ff_n : (d + 1) * ff_n] = mine[2:3, :ff_n]
    for i in range(dp // sp):
        block = small[me * (dp // sp) + i].astype(F32)
        for s in range(sp):
            at = (i * sp + s) * own_b
            jadd[0:1, at : at + own_b] = block[0:1, s * LANES : s * LANES + own_b]


def mlp_kernel(sp, row_n, own_b, ids, *refs):
    xs, cots = refs[:sp], refs[sp : 2 * sp]
    ew_mine, ew_got, sw_mine, sw_got = refs[2 * sp : 2 * sp + 4]
    outs = refs[2 * sp + 4 : 2 * sp + 13]
    eg_keep, eg_send, sg_keep, sg_send, out_part, in_part, sums, vecs, jadd = outs
    x, cot, ew, sw, hid, act, pgr, eg, sg, small, eadd, sem = refs[2 * sp + 13 :]
    width = x.shape[1]
    chunk = x.shape[0] // sp
    rows, units = eg_keep.shape[1], sg_keep.shape[1]
    half = ew_mine.shape[0]
    side = 2 * half + sp + 1
    gets = (
        copies_in([b.at[pl.ds(0, chunk)] for b in xs], x, chunk, sem.at[0])
        + copies_in([b.at[pl.ds(0, chunk)] for b in cots], cot, chunk, sem.at[1])
        + placed(ids, ew_mine, ew_got, ew, rows, ew.shape[1], sem.at[2])
        + placed(ids, sw_mine, sw_got, sw, units, width, sem.at[3])
    )
    for p in range(2 * half):
        block = ew_mine.at[p] if p < half else ew_got.at[p - half]
        block = block.at[pl.ds(ew_mine.shape[1] - 8, 8)]
        gets.append(pltpu.make_async_copy(block, small.at[ids[p]], sem.at[4, p]))
    run(gets)
    sums[...] = jnp.zeros_like(sums)
    jadd[...] = jnp.zeros_like(jadd)
    finish(gets)
    unpack(sp, ids[2 * half + sp], small, row_n, own_b, vecs, eadd, jadd)
    gain, shift, add = vecs[6:7, :], vecs[7:8, :], eadd[...]

    @pl.loop(0, sp)
    def _(k):
        at = pl.ds(pl.multiple_of(k * chunk, chunk), chunk)
        normed, _ = layer_norm(x[at, :].astype(F32))
        hidden = (normed * gain + shift).astype(BF)
        hid[at, :] = hidden
        pre = dot(hidden, ew[...], 1, 0) + add
        cdf = 0.5 * (1.0 + lax.erf(pre * 0.7071067811865476))
        activated = (pre * cdf).astype(BF)
        act[at, :] = activated
        slope = cdf + pre * jnp.exp(-0.5 * pre * pre) * 0.3989422804014327
        pre_grad = dot(cot[at, :], sw[...], 1, 1) * slope
        sums[0:1, : ew.shape[1]] += row_sum(pre_grad)
        pre_grad_bf = pre_grad.astype(BF)
        pgr[at, :] = pre_grad_bf
        out_part[k] = dot(activated, sw[...], 1, 0).astype(BF)
        hidden_grad = dot(pre_grad_bf, ew[...], 1, 1)
        sums[1:2, :] += row_sum(hidden_grad * normed)
        sums[2:3, :] += row_sum(hidden_grad)
        in_part[k] = (hidden_grad * gain).astype(BF)

    grad_rows(hid, pgr, eg)
    puts = sent(ids, eg, eg_keep, eg_send, rows, sem.at[0], side)
    run(puts)
    grad_rows(act, cot, sg)
    more = sent(ids, sg, sg_keep, sg_send, units, sem.at[1])
    run(more)
    finish(puts + more)


def attn_kernel(sp, seqs, heads, ids, *refs):
    xs, cots = refs[:sp], refs[sp : 2 * sp]
    jw_mine, jw_got, dw, cos_ref, sin_ref = refs[2 * sp : 2 * sp + 5]
    out_part, in_part, m_sums, vecs, jadd = refs[2 * sp + 5 : 2 * sp + 10]
    g_keep, g_send, keep, send = refs[2 * sp + 10 : 2 * sp + 14]
    x, cot, jw, hid, rot, cg, ctx, jgf, jgb, ctk, gr, sums, small, sem = refs[2 * sp + 14 :]
    width = x.shape[1]
    wide = jw.shape[1]
    cols = heads * 3 * HD
    chunk = x.shape[0] // sp
    part = chunk // seqs
    full = part * sp
    half = g_keep.shape[0]
    rows = width // (2 * half)
    per = rows // sp
    scale = HD ** (-0.5)
    gets = (
        copies_in([b.at[pl.ds(0, chunk)] for b in xs], x, chunk, sem.at[0])
        + copies_in([b.at[pl.ds(0, chunk)] for b in cots], cot, chunk, sem.at[1])
        + placed(ids, jw_mine, jw_got, jw, rows, wide, sem.at[2])
    )
    run(gets)
    sums[...] = jnp.zeros_like(sums)
    jgf[:, cols:] = jnp.zeros((jgf.shape[0], wide - cols), F32)
    finish(gets)
    gain, shift = vecs[4:5, :], vecs[5:6, :]

    def tables(g, k):
        at = pl.ds(pl.multiple_of(k * part, part), part)
        lane = lax.broadcasted_iota(jnp.int32, (part, LANES), 1)
        col = lane + g * LANES
        inner = col % HD
        turned = (inner < ROT) & ((col // HD) % 3 < 2) & (col < cols)
        cos_val, sin_val = cos_ref[at, :], sin_ref[at, :]
        low = jnp.where(turned & (inner < ROT // 2), sin_val, 0.0)
        high = jnp.where(turned & (inner >= ROT // 2), sin_val, 0.0)
        both = [jnp.where(turned, cos_val, 1.0), low, high]
        return [jnp.concatenate([t] * seqs, axis=0) for t in both]

    def rotate(value, g, k, sign):
        cos_val, low, high = tables(g, k)
        up = pltpu.roll(value, LANES - ROT // 2, 1)
        down = pltpu.roll(value, ROT // 2, 1)
        return value * cos_val + sign * (down * high - up * low)

    def spread(ref, k, lanes, value):
        for b in range(seqs):
            at = pl.ds(pl.multiple_of(b * full + ids[2 * half + k] * part, part), part)
            ref[at, lanes] = value[b * part : (b + 1) * part]

    def collect(ref, k, lanes):
        row = ids[2 * half + k] * part
        at = [pl.ds(pl.multiple_of(b * full + row, part), part) for b in range(seqs)]
        return jnp.concatenate([ref[a, lanes] for a in at], axis=0)

    @pl.loop(0, sp)
    def _(k):
        at = pl.ds(pl.multiple_of(k * chunk, chunk), chunk)
        normed, _ = layer_norm(x[at, :].astype(F32))
        hidden = (normed * gain + shift).astype(BF)
        hid[at, :] = hidden
        joined = dot(hidden, jw[...], 1, 0) + jadd[0:1, :]
        for g in range(wide // LANES):
            lanes = slice(g * LANES, (g + 1) * LANES)
            spread(rot, k, lanes, rotate(joined[:, lanes], g, k, 1.0).astype(BF))
        spread(cg, k, slice(None), dot(cot[at, :], dw[...], 1, 1).astype(BF))

    step = full // SPLITS
    row = lax.broadcasted_iota(jnp.int32, (step, step), 0)
    allowed = row <= lax.broadcasted_iota(jnp.int32, (step, step), 1)

    def stripe(b, i):
        at = pl.ds(pl.multiple_of(b * full + i * step, step), step)
        seen = pl.ds(pl.multiple_of(b * full, full), (i + 1) * step)
        every = range(heads)
        starts = [h * 3 * HD for h in every]
        query = [(rot[at, q : q + HD].astype(F32) * scale).astype(BF) for q in starts]
        key = [rot[seen, q + HD : q + 2 * HD] for q in starts]
        value = [rot[seen, q + 2 * HD : q + 3 * HD] for q in starts]
        grad = [cg[at, h * HD : (h + 1) * HD] for h in every]
        scores = [dot(key[h], query[h], 1, 1) for h in every]
        weight_grad = [dot(value[h], grad[h], 1, 1) for h in every]
        for h in every:
            last = jnp.where(allowed, scores[h][i * step :], -jnp.inf)
            scores[h] = jnp.concatenate([scores[h][: i * step], last], axis=0) if i else last
        total = [row_sum(jnp.exp(scores[h])) for h in every]
        probs = [jnp.exp(scores[h] - jnp.log(total[h])) for h in every]
        weights = [probs[h].astype(BF) for h in every]
        context = [dot(value[h], weights[h], 0, 0) for h in every]
        delta = [row_sum(grad[h].astype(F32).T * context[h]) for h in every]
        inner = [(probs[h] * (weight_grad[h] - delta[h])).astype(BF) for h in every]
        for h in every:
            q = starts[h]
            ctx[at, h * HD : (h + 1) * HD] = context[h].T.astype(BF)
            jgf[at, q : q + HD] = dot(key[h], inner[h], 0, 0).T * scale
            both = [dot(inner[h], query[h], 1, 0), dot(weights[h], grad[h], 1, 0)]
            both = jnp.concatenate(both, axis=1)
            if i == SPLITS - 1:
                jgf[seen, q + HD : q + 3 * HD] = both
            else:
                jgf[seen, q + HD : q + 3 * HD] += both

    @pl.loop(0, seqs)
    def _(b):
        for i in reversed(range(SPLITS)):
            stripe(b, i)

    @pl.loop(0, sp)
    def _(k):
        at = pl.ds(pl.multiple_of(k * chunk, chunk), chunk)
        for g in range(wide // LANES):
            lanes = slice(g * LANES, (g + 1) * LANES)
            back = rotate(collect(jgf, k, lanes), g, k, -1.0).astype(BF)
            jgb[at, lanes] = back
            sums[5:6, lanes] += row_sum(back.astype(F32))
        hidden_grad = dot(jgb[at, :], jw[...], 1, 1)
        normed, _ = layer_norm(x[at, :].astype(F32))
        sums[0:1, :] += row_sum(hidden_grad * normed)
        sums[1:2, :] += row_sum(hidden_grad)
        context = collect(ctx, k, slice(None))
        ctk[at, :] = context
        scaled = (hidden_grad * gain + in_part[k].astype(F32)).astype(BF)
        out_sum = (dot(context, dw[...], 1, 0) + out_part[k].astype(F32)).astype(BF)

        @pl.when(k < sp // 2)
        def _():
            keep[k, 0] = out_sum
            keep[k, 1] = scaled

        @pl.when(k >= sp // 2)
        def _():
            send[k - sp // 2, 0] = out_sum
            send[k - sp // 2, 1] = scaled

    sums[2:4, :] = m_sums[1:3, :]
    sums[4:5, :] = row_sum(cot[0:chunk, :].astype(F32))
    sums[6:7, :] = m_sums[0:1, :]
    small[...] = sums[...].astype(BF)
    puts = []
    for p in range(2 * half):
        to = g_keep.at[p] if p < half else g_send.at[p - half]
        puts.append(pltpu.make_async_copy(small, to.at[pl.ds(rows, 8)], sem.at[1, p]))
    run(puts)
    grad_rows(hid, jgb, gr)
    dense_g = dot(ctk[...], cot[...], 0, 0).astype(BF)
    lanes = width - cols
    for d in range(2 * half):
        for q in range(sp):
            piece = dense_g[d * per : (d + 1) * per, q * lanes : (q + 1) * lanes]
            gr[d * rows + q * per : d * rows + (q + 1) * per, cols:] = piece
    more = sent(ids, gr, g_keep, g_send, rows, sem.at[0])
    run(more)
    finish(puts + more)


ANY = pl.BlockSpec(memory_space=pl.ANY)
IN_VMEM = pl.BlockSpec(memory_space=pltpu.VMEM)
IN_SMEM = pl.BlockSpec(memory_space=pltpu.SMEM)


def call(body, args, specs, outs, out_specs, scratch, flops):
    moved = sum(a.size * a.dtype.itemsize for a in args)
    moved += sum(o.size * o.dtype.itemsize for o in outs)
    return pl.pallas_call(
        body,
        in_specs=specs,
        out_shape=outs,
        out_specs=out_specs,
        scratch_shapes=scratch,
        compiler_params=pltpu.CompilerParams(vmem_limit_bytes=VMEM_LIMIT),
        cost_estimate=pl.CostEstimate(flops=flops, bytes_accessed=moved, transcendentals=0),
    )(*args)


def tidy(body, args, outs):
    specs = [IN_SMEM if a.dtype == jnp.int32 else IN_VMEM for a in args]
    return call(body, args, specs, outs, [IN_VMEM] * len(outs), [], 0)


def split_weights(sp, dp, expand, joined, *refs):
    vectors, out = refs[:-1], refs[-1]
    rows = expand.shape[0]
    each = expand.shape[1] // (sp * dp)
    cols = joined.shape[1] // sp
    for s in range(sp):
        for d in range(dp):
            at = (d * sp + s) * each
            out[s, :rows, d * each : (d + 1) * each] = expand[:, at : at + each]
        out[s, rows : 2 * rows, :cols] = joined[:, s * cols : (s + 1) * cols]
        out[s, rows : 2 * rows, cols:] = jnp.zeros((rows, out.shape[2] - cols), out.dtype)
        out[s, 2 * rows :, :] = jnp.zeros((8, out.shape[2]), out.dtype)
        for i, vector in enumerate(vectors):
            out[s, 2 * rows + i : 2 * rows + i + 1, : vector.shape[0]] = vector[...][None, :]


def pack_weights(wide, both, pack, joined):
    sp = both.shape[0]
    rows = joined.shape[0] // sp
    pack[sp * rows :, :] = jnp.zeros((8, pack.shape[1]), pack.dtype)
    for s in range(sp):
        pack[s * rows : (s + 1) * rows, :] = both[s, :rows]
        joined[s * rows : (s + 1) * rows, :] = both[s, rows : 2 * rows, :wide]
        pack[sp * rows :, s * LANES : (s + 1) * LANES] = both[s, 2 * rows :, :LANES]


def split_grads(sp, cols, keep, got, e_keep, e_got, last, dense):
    value = (keep[...] + got[...].astype(F32)).astype(BF)
    expand = (e_keep[...] + e_got[...].astype(F32)).astype(BF)
    rows = value.shape[0] - 8
    per = rows // sp
    lanes = value.shape[1] - cols
    for s in range(sp):
        last[s, :per] = value[s * per : (s + 1) * per]
        last[s, per : 2 * per] = expand[s * per : (s + 1) * per]
        last[s, 2 * per :] = value[rows:]
        dense[:, s * lanes : (s + 1) * lanes] = value[s * per : (s + 1) * per, cols:]


def join_grads(sp, dp, cols, at, last, out, expand, *vectors):
    per = out.shape[0]
    width = last.shape[2]
    each = width // dp
    total = jnp.zeros((8, width), F32)
    joined = jnp.zeros((8, width), F32)
    for s in range(sp):
        out[:, s * cols : (s + 1) * cols] = last[s, :per, :cols].astype(F32)
        for d in range(dp):
            to = (d * sp + s) * each
            expand[:, to : to + each] = last[s, per : 2 * per, d * each : (d + 1) * each].astype(F32)
        block = last[s, 2 * per :].astype(F32)
        total = total + block
        joined = joined + jnp.where(at[0] == s, block, 0.0)
    mine = last[at[4], 2 * per :].astype(F32)
    sums = pltpu.roll(total, at[1], 1)[:, :LANES]
    joined = pltpu.roll(joined, at[2], 1)[:, :LANES]
    mine = pltpu.roll(mine, at[3], 1)[:, :LANES]
    for i, vector in enumerate(vectors):
        source = (sums,) * 5 + (joined, mine, sums)
        vector[...] = source[i][i if i < 7 else 4, : vector.shape[0]]


def finish_tokens(x, cot, keep, got, add, out, grad):
    rows = x[...].astype(F32)
    sums = keep[...].astype(F32) + got[...].astype(F32)
    out[...] = (rows + sums[0] + (add[1:2, :] + add[3:4, :])).astype(BF)
    scaled = sums[1]
    normed, inv = layer_norm(rows)
    first = jnp.mean(scaled, axis=-1, keepdims=True)
    second = jnp.mean(scaled * normed, axis=-1, keepdims=True)
    grad[...] = cot[...].astype(F32) + inv * (scaled - first - normed * second)


def attention(ids, xs, cots, jw, dw, tables, parts, seqs, heads):
    sp = len(xs)
    chunk, width = parts[0].shape[1:]
    tokens = sp * chunk
    wide = jw[0].shape[2]
    dp = 2 * jw[0].shape[0]
    rows = width // dp
    shape = jax.ShapeDtypeStruct
    outs = [
        shape((dp // 2, rows + 8, width), BF),
        shape((dp // 2, rows + 8, width), BF),
        shape((sp // 2, 2, chunk, width), BF),
        shape((sp // 2, 2, chunk, width), BF),
    ]
    scratch = [
        pltpu.VMEM((tokens, width), BF),
        pltpu.VMEM((tokens, width), BF),
        pltpu.VMEM((width, wide), BF),
        pltpu.VMEM((tokens, width), BF),
        pltpu.VMEM((tokens, wide), BF),
        pltpu.VMEM((tokens, heads * HD), BF),
        pltpu.VMEM((tokens, heads * HD), BF),
        pltpu.VMEM((tokens, wide), F32),
        pltpu.VMEM((tokens, wide), BF),
        pltpu.VMEM((tokens, heads * HD), BF),
        pltpu.VMEM((width, width), BF),
        pltpu.VMEM((8, width), F32),
        pltpu.VMEM((8, width), BF),
        pltpu.SemaphoreType.DMA((3, max(dp, sp))),
    ]
    return call(
        functools.partial(attn_kernel, sp, seqs, heads),
        [ids, *xs, *cots, *jw, dw, *tables, *parts],
        [IN_SMEM] + [ANY] * (2 * sp + 2) + [IN_VMEM] * 8,
        outs,
        [ANY, ANY, IN_VMEM, IN_VMEM],
        scratch,
        24 * tokens * width * wide,
    )


def feed_forward(ids, xs, cots, ew, sw, row_n, own_b, wide):
    sp = len(xs)
    chunk, width = xs[0].shape
    tokens = sp * chunk
    units = ew[0].shape[2]
    dp = 2 * ew[0].shape[0]
    rows, per = width // dp, units // dp
    shape = jax.ShapeDtypeStruct
    outs = [
        shape((dp // 2, rows, units), BF),
        shape((dp // 2, rows, units), BF),
        shape((dp // 2, per, width), BF),
        shape((dp // 2, per, width), BF),
        shape((sp, chunk, width), BF),
        shape((sp, chunk, width), BF),
        shape((8, width), F32),
        shape((8, width), F32),
        shape((8, wide), F32),
    ]
    scratch = [
        pltpu.VMEM((tokens, width), BF),
        pltpu.VMEM((tokens, width), BF),
        pltpu.VMEM((width, units), BF),
        pltpu.VMEM((units, width), BF),
        pltpu.VMEM((tokens, width), BF),
        pltpu.VMEM((tokens, units), BF),
        pltpu.VMEM((tokens, units), BF),
        pltpu.VMEM((width, units), BF),
        pltpu.VMEM((units, width), BF),
        pltpu.VMEM((dp, 8, width), BF),
        pltpu.VMEM((1, units), F32),
        pltpu.SemaphoreType.DMA((5, max(dp, sp))),
    ]
    return call(
        functools.partial(mlp_kernel, sp, row_n, own_b),
        [ids, *xs, *cots, *ew, *sw],
        [IN_SMEM] + [ANY] * (2 * sp + 4),
        outs,
        [ANY, ANY, ANY, ANY] + [IN_VMEM] * 5,
        scratch,
        20 * tokens * width * units,
    )


def on_device(
    inputs,
    cotangent,
    joined_weight,
    joined_bias,
    dense_weight,
    dense_bias,
    expand_weight,
    expand_bias,
    shrink_weight,
    shrink_bias,
    attn_gain,
    attn_shift,
    mlp_gain,
    mlp_shift,
):
    seqs, local_len, width = inputs.shape
    sp, dp = lax.axis_size("sp"), lax.axis_size("dp")
    me, dp_me = lax.axis_index("sp"), lax.axis_index("dp")
    heads = HEADS // sp
    local = seqs * local_len
    cols = joined_weight.shape[1] // sp
    wide = -(-cols // LANES) * LANES
    row_n = joined_weight.shape[0]
    rows_d = row_n * sp
    ff_n = shrink_weight.shape[0]
    units = ff_n * dp
    sp_order = cube_order(bits_of(sp))
    dp_order, side_order = cube_order(bits_of(dp)), cube_order(side_first(dp))
    nat = jnp.asarray(sp_order, jnp.int32) ^ me
    near = jnp.asarray(dp_order, jnp.int32) ^ dp_me
    side = jnp.asarray(side_order, jnp.int32) ^ dp_me
    ids = jnp.concatenate([near, nat, me[None], side])
    own_b = joined_bias.shape[0]

    small_parts = (
        joined_bias,
        dense_bias,
        expand_bias,
        shrink_bias,
        attn_gain,
        attn_shift,
        mlp_gain,
        mlp_shift,
    )
    shape = jax.ShapeDtypeStruct
    (both,) = tidy(
        functools.partial(split_weights, sp, dp),
        [expand_weight, joined_weight, *small_parts],
        [shape((sp, 2 * row_n + 8, units), BF)],
    )
    both = lax.all_to_all(both, "sp", split_axis=0, concat_axis=0, tiled=True)
    dense_part = transposed(dense_weight, False)
    expand_pack, joined_part = tidy(
        functools.partial(pack_weights, wide),
        [both],
        [shape((rows_d + 8, units), BF), shape((rows_d, wide), BF)],
    )

    xs = token_blocks(inputs.reshape(local, width), "sp")
    cots = token_blocks(cotangent.reshape(local, width), "sp")
    shrink_w = halves(shrink_weight, "dp", bits_of(dp))
    expand_w = halves(expand_pack, "dp", bits_of(dp))
    joined_w = halves(joined_part, "dp", bits_of(dp))
    dense_w = jnp.concatenate(halves(dense_part, "dp", bits_of(dp)), axis=0)
    dense_w = flip_bits(turn_bits(dense_w), "dp").reshape(heads * HD, width)
    pos = (nat[:, None] * local_len + jnp.arange(local_len, dtype=jnp.int32)).reshape(-1)
    lane = jnp.arange(LANES, dtype=jnp.int32) % (ROT // 2)
    freq = 1.0 / 10000.0 ** ((2 * lane).astype(F32) / ROT)
    angles = pos.astype(F32)[:, None] * freq[None, :]
    e_keep, e_send, s_keep, s_send, *parts = feed_forward(
        ids,
        xs,
        cots,
        expand_w,
        shrink_w,
        row_n,
        own_b,
        wide,
    )
    a_keep, a_send, keep, send = attention(
        ids,
        xs,
        cots,
        joined_w,
        dense_w,
        (jnp.cos(angles), jnp.sin(angles)),
        parts,
        seqs,
        heads,
    )

    keep, got = cube_scatter(keep, send, "sp", bits_of(sp))
    output, input_grad = tidy(
        finish_tokens,
        [
            inputs.reshape(local, width),
            cotangent.reshape(local, width),
            keep,
            got,
            parts[3],
        ],
        [shape((local, width), BF), shape((local, width), F32)],
    )
    output, input_grad = output.reshape(inputs.shape), input_grad.reshape(inputs.shape)

    keep, got = cube_scatter(s_keep, s_send, "dp", bits_of(dp))
    shrink_g = keep + got.astype(F32)
    keep, got = cube_scatter(e_keep, e_send, "dp", side_first(dp))
    expands = (keep, got)
    keep, got = cube_scatter(a_keep, a_send, "dp", bits_of(dp))
    last, dense_g = tidy(
        functools.partial(split_grads, sp, cols),
        [keep, got, *expands],
        [shape((sp, 2 * row_n + 8, width), BF), shape((row_n, width), BF)],
    )
    last = lax.all_to_all(last, "sp", split_axis=0, concat_axis=0, tiled=True)
    dense_g = transposed(dense_g, True)
    linear = dp_me * sp + me
    holder = linear * own_b // cols
    starts = [linear * row_n, linear * own_b - holder * cols, dp_me * ff_n]
    at = [holder] + [(width - start) % width for start in starts] + [me]
    joined_g, expand_g, *vectors = tidy(
        functools.partial(join_grads, sp, dp, cols),
        [jnp.stack(at).astype(jnp.int32), last],
        [shape(joined_weight.shape, F32), shape(expand_weight.shape, F32)]
        + [shape((n,), F32) for n in [row_n] * 5 + [own_b, ff_n, row_n]],
    )
    gain_ag, shift_ag, gain_bg, shift_bg, dense_bg, joined_bg, expand_bg, shrink_bg = vectors
    return (
        output,
        input_grad,
        joined_g,
        joined_bg,
        dense_g.astype(F32),
        dense_bg,
        expand_g,
        expand_bg,
        shrink_g,
        shrink_bg,
        gain_ag,
        shift_ag,
        gain_bg,
        shift_bg,
    )


def solution(mesh):
    token = P("dp", "sp", None)
    matrix = P(("dp", "sp"), None)
    vector = P(("dp", "sp"))
    params = (matrix, vector) * 4 + (vector,) * 4
    return jax.shard_map(
        on_device,
        mesh=mesh,
        in_specs=(token, token) + params,
        out_specs=(token, token) + params,
        check_vma=False,
    )
```

```python
import functools

import jax
import jax.numpy as jnp
from jax import lax
from jax.experimental import pallas as pl
from jax.experimental.pallas import tpu as pltpu
from jax.sharding import PartitionSpec as P


HEADS = 12
HD = 64
ROT = 16
LANES = 128
SPLITS = 2
NORM_EPS = 1e-05
BF = jnp.bfloat16
F32 = jnp.float32
VMEM_LIMIT = 60 * 1024 * 1024


def bits_of(count):
    assert count & (count - 1) == 0
    bit = 1
    out = []
    while bit < count:
        out.append(bit)
        bit *= 2
    return out


def cube_order(bits):
    order = [0]
    for bit in reversed(bits):
        order = order + [k ^ bit for k in order]
    return order


def side_first(count):
    bits = bits_of(count)
    return [bits[1], bits[0], *bits[2:]]


def swap(value, axis, bit):
    count = lax.axis_size(axis)
    return lax.ppermute(value, axis, [(i, i ^ bit) for i in range(count)])


def halves(block, axis, bits):
    mine, got = None, block[None]
    for bit in reversed(bits):
        mine = got if mine is None else jnp.concatenate([mine, got], axis=0)
        got = swap(mine, axis, bit)
    return mine, got


def pieces(block, axis, bits):
    parts = [block[None]]
    for bit in reversed(bits[1:]):
        parts.append(swap(jnp.concatenate(parts, axis=0), axis, bit))
    early = swap(parts[0], axis, bits[0])
    rest = swap(jnp.concatenate(parts[1:], axis=0), axis, bits[0])
    return [*parts, early, rest]


def token_blocks(block, axis):
    blocks = [block]
    for bit in reversed(bits_of(lax.axis_size(axis))):
        more = []
        for b in blocks:
            more.append(swap(b, axis, bit))
        blocks = blocks + more
    return blocks


def transposed(value, back):
    dp, sp = lax.axis_size("dp"), lax.axis_size("sp")
    perm = [(s * dp + b, b * sp + s) for s in range(sp) for b in range(dp)]
    if back:
        perm = [(to, at) for at, to in perm]
    return lax.ppermute(value, ("dp", "sp"), perm)


def cube_scatter(keep, send, axis, bits):
    for bit in bits:
        got = swap(send, axis, bit)
        half = keep.shape[0] // 2
        if half:
            send = (keep[half:].astype(F32) + got[half:].astype(F32)).astype(BF)
            keep = keep[:half].astype(F32) + got[:half].astype(F32)
    return keep[0], got[0]


def flip_bits(blocks, axis):
    count = lax.axis_size(axis)
    me = lax.axis_index(axis)
    rest = blocks.shape[1:]
    for bit in bits_of(count):
        pairs = blocks.reshape((count // (2 * bit), 2, bit) + rest)
        blocks = jnp.where((me & bit) > 0, pairs[:, ::-1], pairs).reshape((count,) + rest)
    return blocks


def turn_bits(blocks):
    count = blocks.shape[0]
    bits = len(bits_of(count))
    rest = blocks.shape[1:]
    blocks = blocks.reshape((2,) * bits + rest)
    axes = tuple(reversed(range(bits))) + tuple(range(bits, bits + len(rest)))
    return blocks.transpose(axes).reshape((count,) + rest)


def layer_norm(values):
    mean_val = jnp.mean(values, axis=-1, keepdims=True)
    centred = values - mean_val
    variance = jnp.mean(centred * centred, axis=-1, keepdims=True)
    inv_std = lax.rsqrt(variance + NORM_EPS)
    return centred * inv_std, inv_std


def dot(left, right, left_dim, right_dim):
    dims = (((left_dim,), (right_dim,)), ((), ()))
    return lax.dot_general(left, right, dims, preferred_element_type=F32)


def row_sum(value):
    return jnp.sum(value, axis=0, keepdims=True)


def copies_in(blocks, target, rows, sem):
    out = []
    for i, block in enumerate(blocks):
        out.append(pltpu.make_async_copy(block, target.at[pl.ds(i * rows, rows)], sem.at[i]))
    return out


def blocks_of(stacks):
    return [stack.at[i] for stack in stacks for i in range(stack.shape[0])]


def placed(ids, stacks, target, rows, width, sem):
    out = []
    for p, source in enumerate(blocks_of(stacks)):
        if source.shape != (rows, width):
            source = source.at[pl.ds(0, rows), pl.ds(0, width)]
        to = pl.multiple_of(ids[p] * rows, 8)
        out.append(pltpu.make_async_copy(source, target.at[pl.ds(to, rows)], sem.at[p]))
    return out


def sent(ids, source, keep, send, rows, sem, first=0):
    todo = []
    half = keep.shape[0]
    for p in range(2 * half):
        at = pl.multiple_of(ids[first + p] * rows, 8)
        to = keep.at[p] if p < half else send.at[p - half]
        if to.shape[0] != rows:
            to = to.at[pl.ds(0, rows)]
        todo.append(pltpu.make_async_copy(source.at[pl.ds(at, rows)], to, sem.at[p]))
    return todo


def run(copies):
    for copy in copies:
        copy.start()


def finish(copies):
    for copy in copies:
        copy.wait()


def grad_rows(left, right, out):
    rows = 256

    @pl.loop(0, left.shape[1] // rows)
    def _(r):
        at = pl.ds(pl.multiple_of(r * rows, rows), rows)
        out[at, : right.shape[1]] = dot(left[:, at], right[...], 0, 0).astype(BF)


def unpack(sp, me, small, row_n, own_b, vecs, eadd, jadd):
    dp = small.shape[0]
    ff_n = eadd.shape[1] // dp
    for d in range(dp):
        block = small[d].astype(F32)
        for s in range(sp):
            at = (d * sp + s) * row_n
            vecs[:, at : at + row_n] = block[:, s * LANES : s * LANES + row_n]
        lanes = pl.ds(pl.multiple_of(me * LANES, LANES), LANES)
        mine = small[d, :, lanes].astype(F32)
        eadd[:, d * ff_n : (d + 1) * ff_n] = mine[2:3, :ff_n]
    for i in range(dp // sp):
        block = small[me * (dp // sp) + i].astype(F32)
        for s in range(sp):
            at = (i * sp + s) * own_b
            jadd[0:1, at : at + own_b] = block[0:1, s * LANES : s * LANES + own_b]


def mlp_kernel(sp, row_n, own_b, stacks, ids, *refs):
    xs, cots = refs[:sp], refs[sp : 2 * sp]
    refs, ew_in, sw_in = refs[2 * sp :], refs[2 * sp : 2 * sp + stacks], refs[2 * sp + stacks :]
    sw_in, refs = sw_in[:stacks], refs[2 * stacks :]
    outs = refs[:9]
    eg_keep, eg_send, sg_keep, sg_send, out_part, in_part, sums, vecs, jadd = outs
    x, cot, ew, sw, hid, act, pgr, eg, sg, small, eadd, sem = refs[9:]
    width = x.shape[1]
    chunk = x.shape[0] // sp
    rows, units = eg_keep.shape[1], sg_keep.shape[1]
    dp = small.shape[0]
    side = dp + sp + 1
    gets = (
        copies_in([b.at[pl.ds(0, chunk)] for b in xs], x, chunk, sem.at[0])
        + copies_in([b.at[pl.ds(0, chunk)] for b in cots], cot, chunk, sem.at[1])
        + placed(ids, ew_in, ew, rows, ew.shape[1], sem.at[2])
        + placed(ids, sw_in, sw, units, width, sem.at[3])
    )
    for p, block in enumerate(blocks_of(ew_in)):
        block = block.at[pl.ds(block.shape[0] - 8, 8)]
        gets.append(pltpu.make_async_copy(block, small.at[ids[p]], sem.at[4, p]))
    run(gets)
    sums[...] = jnp.zeros_like(sums)
    jadd[...] = jnp.zeros_like(jadd)
    finish(gets)
    unpack(sp, ids[dp + sp], small, row_n, own_b, vecs, eadd, jadd)
    gain, shift, add = vecs[6:7, :], vecs[7:8, :], eadd[...]

    @pl.loop(0, sp)
    def _(k):
        at = pl.ds(pl.multiple_of(k * chunk, chunk), chunk)
        normed, _ = layer_norm(x[at, :].astype(F32))
        hidden = (normed * gain + shift).astype(BF)
        hid[at, :] = hidden
        pre = dot(hidden, ew[...], 1, 0) + add
        cdf = 0.5 * (1.0 + lax.erf(pre * 0.7071067811865476))
        activated = (pre * cdf).astype(BF)
        act[at, :] = activated
        slope = cdf + pre * jnp.exp(-0.5 * pre * pre) * 0.3989422804014327
        pre_grad = dot(cot[at, :], sw[...], 1, 1) * slope
        sums[0:1, : ew.shape[1]] += row_sum(pre_grad)
        pre_grad_bf = pre_grad.astype(BF)
        pgr[at, :] = pre_grad_bf
        out_part[k] = dot(activated, sw[...], 1, 0).astype(BF)
        hidden_grad = dot(pre_grad_bf, ew[...], 1, 1)
        sums[1:2, :] += row_sum(hidden_grad * normed)
        sums[2:3, :] += row_sum(hidden_grad)
        in_part[k] = (hidden_grad * gain).astype(BF)

    grad_rows(hid, pgr, eg)
    puts = sent(ids, eg, eg_keep, eg_send, rows, sem.at[0], side)
    run(puts)
    grad_rows(act, cot, sg)
    more = sent(ids, sg, sg_keep, sg_send, units, sem.at[1])
    run(more)
    finish(puts + more)


def attn_kernel(sp, seqs, heads, ids, *refs):
    xs, cots = refs[:sp], refs[sp : 2 * sp]
    jw_mine, jw_got, dw, cos_ref, sin_ref = refs[2 * sp : 2 * sp + 5]
    out_part, in_part, m_sums, vecs, jadd = refs[2 * sp + 5 : 2 * sp + 10]
    g_keep, g_send, keep, send = refs[2 * sp + 10 : 2 * sp + 14]
    x, cot, jw, hid, rot, cg, ctx, jgf, jgb, ctk, gr, sums, small, sem = refs[2 * sp + 14 :]
    width = x.shape[1]
    wide = jw.shape[1]
    cols = heads * 3 * HD
    chunk = x.shape[0] // sp
    part = chunk // seqs
    full = part * sp
    half = g_keep.shape[0]
    rows = width // (2 * half)
    per = rows // sp
    scale = HD ** (-0.5)
    gets = (
        copies_in([b.at[pl.ds(0, chunk)] for b in xs], x, chunk, sem.at[0])
        + copies_in([b.at[pl.ds(0, chunk)] for b in cots], cot, chunk, sem.at[1])
        + placed(ids, (jw_mine, jw_got), jw, rows, wide, sem.at[2])
    )
    run(gets)
    sums[...] = jnp.zeros_like(sums)
    jgf[:, cols:] = jnp.zeros((jgf.shape[0], wide - cols), F32)
    finish(gets)
    gain, shift = vecs[4:5, :], vecs[5:6, :]

    def tables(g, k):
        at = pl.ds(pl.multiple_of(k * part, part), part)
        lane = lax.broadcasted_iota(jnp.int32, (part, LANES), 1)
        col = lane + g * LANES
        inner = col % HD
        turned = (inner < ROT) & ((col // HD) % 3 < 2) & (col < cols)
        cos_val, sin_val = cos_ref[at, :], sin_ref[at, :]
        low = jnp.where(turned & (inner < ROT // 2), sin_val, 0.0)
        high = jnp.where(turned & (inner >= ROT // 2), sin_val, 0.0)
        both = [jnp.where(turned, cos_val, 1.0), low, high]
        return [jnp.concatenate([t] * seqs, axis=0) for t in both]

    def rotate(value, g, k, sign):
        cos_val, low, high = tables(g, k)
        up = pltpu.roll(value, LANES - ROT // 2, 1)
        down = pltpu.roll(value, ROT // 2, 1)
        return value * cos_val + sign * (down * high - up * low)

    def spread(ref, k, lanes, value):
        for b in range(seqs):
            at = pl.ds(pl.multiple_of(b * full + ids[2 * half + k] * part, part), part)
            ref[at, lanes] = value[b * part : (b + 1) * part]

    def collect(ref, k, lanes):
        row = ids[2 * half + k] * part
        at = [pl.ds(pl.multiple_of(b * full + row, part), part) for b in range(seqs)]
        return jnp.concatenate([ref[a, lanes] for a in at], axis=0)

    @pl.loop(0, sp)
    def _(k):
        at = pl.ds(pl.multiple_of(k * chunk, chunk), chunk)
        normed, _ = layer_norm(x[at, :].astype(F32))
        hidden = (normed * gain + shift).astype(BF)
        hid[at, :] = hidden
        joined = dot(hidden, jw[...], 1, 0) + jadd[0:1, :]
        for g in range(wide // LANES):
            lanes = slice(g * LANES, (g + 1) * LANES)
            spread(rot, k, lanes, rotate(joined[:, lanes], g, k, 1.0).astype(BF))
        spread(cg, k, slice(None), dot(cot[at, :], dw[...], 1, 1).astype(BF))

    step = full // SPLITS
    row = lax.broadcasted_iota(jnp.int32, (step, step), 0)
    allowed = row <= lax.broadcasted_iota(jnp.int32, (step, step), 1)

    def stripe(b, i):
        at = pl.ds(pl.multiple_of(b * full + i * step, step), step)
        seen = pl.ds(pl.multiple_of(b * full, full), (i + 1) * step)
        every = range(heads)
        starts = [h * 3 * HD for h in every]
        query = [(rot[at, q : q + HD].astype(F32) * scale).astype(BF) for q in starts]
        key = [rot[seen, q + HD : q + 2 * HD] for q in starts]
        value = [rot[seen, q + 2 * HD : q + 3 * HD] for q in starts]
        grad = [cg[at, h * HD : (h + 1) * HD] for h in every]
        scores = [dot(key[h], query[h], 1, 1) for h in every]
        weight_grad = [dot(value[h], grad[h], 1, 1) for h in every]
        for h in every:
            last = jnp.where(allowed, scores[h][i * step :], -jnp.inf)
            scores[h] = jnp.concatenate([scores[h][: i * step], last], axis=0) if i else last
        total = [row_sum(jnp.exp(scores[h])) for h in every]
        probs = [jnp.exp(scores[h] - jnp.log(total[h])) for h in every]
        weights = [probs[h].astype(BF) for h in every]
        context = [dot(value[h], weights[h], 0, 0) for h in every]
        delta = [row_sum(grad[h].astype(F32).T * context[h]) for h in every]
        inner = [(probs[h] * (weight_grad[h] - delta[h])).astype(BF) for h in every]
        for h in every:
            q = starts[h]
            ctx[at, h * HD : (h + 1) * HD] = context[h].T.astype(BF)
            jgf[at, q : q + HD] = dot(key[h], inner[h], 0, 0).T * scale
            both = [dot(inner[h], query[h], 1, 0), dot(weights[h], grad[h], 1, 0)]
            both = jnp.concatenate(both, axis=1)
            if i == SPLITS - 1:
                jgf[seen, q + HD : q + 3 * HD] = both
            else:
                jgf[seen, q + HD : q + 3 * HD] += both

    @pl.loop(0, seqs)
    def _(b):
        for i in reversed(range(SPLITS)):
            stripe(b, i)

    @pl.loop(0, sp)
    def _(k):
        at = pl.ds(pl.multiple_of(k * chunk, chunk), chunk)
        for g in range(wide // LANES):
            lanes = slice(g * LANES, (g + 1) * LANES)
            back = rotate(collect(jgf, k, lanes), g, k, -1.0).astype(BF)
            jgb[at, lanes] = back
            sums[5:6, lanes] += row_sum(back.astype(F32))
        hidden_grad = dot(jgb[at, :], jw[...], 1, 1)
        normed, _ = layer_norm(x[at, :].astype(F32))
        sums[0:1, :] += row_sum(hidden_grad * normed)
        sums[1:2, :] += row_sum(hidden_grad)
        context = collect(ctx, k, slice(None))
        ctk[at, :] = context
        scaled = (hidden_grad * gain + in_part[k].astype(F32)).astype(BF)
        out_sum = (dot(context, dw[...], 1, 0) + out_part[k].astype(F32)).astype(BF)

        @pl.when(k < sp // 2)
        def _():
            keep[k, 0] = out_sum
            keep[k, 1] = scaled

        @pl.when(k >= sp // 2)
        def _():
            send[k - sp // 2, 0] = out_sum
            send[k - sp // 2, 1] = scaled

    sums[2:4, :] = m_sums[1:3, :]
    sums[4:5, :] = row_sum(cot[0:chunk, :].astype(F32))
    sums[6:7, :] = m_sums[0:1, :]
    small[...] = sums[...].astype(BF)
    puts = []
    for p in range(2 * half):
        to = g_keep.at[p] if p < half else g_send.at[p - half]
        puts.append(pltpu.make_async_copy(small, to.at[pl.ds(rows, 8)], sem.at[1, p]))
    run(puts)
    grad_rows(hid, jgb, gr)
    dense_g = dot(ctk[...], cot[...], 0, 0).astype(BF)
    lanes = width - cols
    for d in range(2 * half):
        for q in range(sp):
            piece = dense_g[d * per : (d + 1) * per, q * lanes : (q + 1) * lanes]
            gr[d * rows + q * per : d * rows + (q + 1) * per, cols:] = piece
    more = sent(ids, gr, g_keep, g_send, rows, sem.at[0])
    run(more)
    finish(puts + more)


ANY = pl.BlockSpec(memory_space=pl.ANY)
IN_VMEM = pl.BlockSpec(memory_space=pltpu.VMEM)
IN_SMEM = pl.BlockSpec(memory_space=pltpu.SMEM)


def call(body, args, specs, outs, out_specs, scratch, flops):
    moved = sum(a.size * a.dtype.itemsize for a in args)
    moved += sum(o.size * o.dtype.itemsize for o in outs)
    return pl.pallas_call(
        body,
        in_specs=specs,
        out_shape=outs,
        out_specs=out_specs,
        scratch_shapes=scratch,
        compiler_params=pltpu.CompilerParams(vmem_limit_bytes=VMEM_LIMIT),
        cost_estimate=pl.CostEstimate(flops=flops, bytes_accessed=moved, transcendentals=0),
    )(*args)


def tidy(body, args, outs):
    specs = [IN_SMEM if a.dtype == jnp.int32 else IN_VMEM for a in args]
    return call(body, args, specs, outs, [IN_VMEM] * len(outs), [], 0)


def split_weights(sp, dp, expand, joined, *refs):
    vectors, out = refs[:-1], refs[-1]
    rows = expand.shape[0]
    each = expand.shape[1] // (sp * dp)
    cols = joined.shape[1] // sp
    for s in range(sp):
        for d in range(dp):
            at = (d * sp + s) * each
            out[s, :rows, d * each : (d + 1) * each] = expand[:, at : at + each]
        out[s, rows : 2 * rows, :cols] = joined[:, s * cols : (s + 1) * cols]
        out[s, rows : 2 * rows, cols:] = jnp.zeros((rows, out.shape[2] - cols), out.dtype)
        out[s, 2 * rows :, :] = jnp.zeros((8, out.shape[2]), out.dtype)
        for i, vector in enumerate(vectors):
            out[s, 2 * rows + i : 2 * rows + i + 1, : vector.shape[0]] = vector[...][None, :]


def pack_weights(wide, both, pack, joined):
    sp = both.shape[0]
    rows = joined.shape[0] // sp
    pack[sp * rows :, :] = jnp.zeros((8, pack.shape[1]), pack.dtype)
    for s in range(sp):
        pack[s * rows : (s + 1) * rows, :] = both[s, :rows]
        joined[s * rows : (s + 1) * rows, :] = both[s, rows : 2 * rows, :wide]
        pack[sp * rows :, s * LANES : (s + 1) * LANES] = both[s, 2 * rows :, :LANES]


def split_grads(sp, cols, keep, got, e_keep, e_got, last, dense):
    value = (keep[...] + got[...].astype(F32)).astype(BF)
    expand = (e_keep[...] + e_got[...].astype(F32)).astype(BF)
    rows = value.shape[0] - 8
    per = rows // sp
    lanes = value.shape[1] - cols
    for s in range(sp):
        last[s, :per] = value[s * per : (s + 1) * per]
        last[s, per : 2 * per] = expand[s * per : (s + 1) * per]
        last[s, 2 * per :] = value[rows:]
        dense[:, s * lanes : (s + 1) * lanes] = value[s * per : (s + 1) * per, cols:]


def join_grads(sp, dp, cols, at, last, out, expand, *vectors):
    per = out.shape[0]
    width = last.shape[2]
    each = width // dp
    total = jnp.zeros((8, width), F32)
    joined = jnp.zeros((8, width), F32)
    for s in range(sp):
        out[:, s * cols : (s + 1) * cols] = last[s, :per, :cols].astype(F32)
        for d in range(dp):
            to = (d * sp + s) * each
            expand[:, to : to + each] = last[s, per : 2 * per, d * each : (d + 1) * each].astype(F32)
        block = last[s, 2 * per :].astype(F32)
        total = total + block
        joined = joined + jnp.where(at[0] == s, block, 0.0)
    mine = last[at[4], 2 * per :].astype(F32)
    sums = pltpu.roll(total, at[1], 1)[:, :LANES]
    joined = pltpu.roll(joined, at[2], 1)[:, :LANES]
    mine = pltpu.roll(mine, at[3], 1)[:, :LANES]
    for i, vector in enumerate(vectors):
        source = (sums,) * 5 + (joined, mine, sums)
        vector[...] = source[i][i if i < 7 else 4, : vector.shape[0]]


def finish_tokens(x, cot, keep, got, add, out, grad):
    rows = x[...].astype(F32)
    sums = keep[...].astype(F32) + got[...].astype(F32)
    out[...] = (rows + sums[0] + (add[1:2, :] + add[3:4, :])).astype(BF)
    scaled = sums[1]
    normed, inv = layer_norm(rows)
    first = jnp.mean(scaled, axis=-1, keepdims=True)
    second = jnp.mean(scaled * normed, axis=-1, keepdims=True)
    grad[...] = cot[...].astype(F32) + inv * (scaled - first - normed * second)


def attention(ids, xs, cots, jw, dw, tables, parts, seqs, heads):
    sp = len(xs)
    chunk, width = parts[0].shape[1:]
    tokens = sp * chunk
    wide = jw[0].shape[2]
    dp = 2 * jw[0].shape[0]
    rows = width // dp
    shape = jax.ShapeDtypeStruct
    outs = [
        shape((dp // 2, rows + 8, width), BF),
        shape((dp // 2, rows + 8, width), BF),
        shape((sp // 2, 2, chunk, width), BF),
        shape((sp // 2, 2, chunk, width), BF),
    ]
    scratch = [
        pltpu.VMEM((tokens, width), BF),
        pltpu.VMEM((tokens, width), BF),
        pltpu.VMEM((width, wide), BF),
        pltpu.VMEM((tokens, width), BF),
        pltpu.VMEM((tokens, wide), BF),
        pltpu.VMEM((tokens, heads * HD), BF),
        pltpu.VMEM((tokens, heads * HD), BF),
        pltpu.VMEM((tokens, wide), F32),
        pltpu.VMEM((tokens, wide), BF),
        pltpu.VMEM((tokens, heads * HD), BF),
        pltpu.VMEM((width, width), BF),
        pltpu.VMEM((8, width), F32),
        pltpu.VMEM((8, width), BF),
        pltpu.SemaphoreType.DMA((3, max(dp, sp))),
    ]
    return call(
        functools.partial(attn_kernel, sp, seqs, heads),
        [ids, *xs, *cots, *jw, dw, *tables, *parts],
        [IN_SMEM] + [ANY] * (2 * sp + 2) + [IN_VMEM] * 8,
        outs,
        [ANY, ANY, IN_VMEM, IN_VMEM],
        scratch,
        24 * tokens * width * wide,
    )


def feed_forward(ids, xs, cots, ew, sw, row_n, own_b, wide):
    sp = len(xs)
    chunk, width = xs[0].shape
    tokens = sp * chunk
    units = ew[0].shape[2]
    dp = sum(stack.shape[0] for stack in ew)
    rows, per = width // dp, units // dp
    shape = jax.ShapeDtypeStruct
    outs = [
        shape((dp // 2, rows, units), BF),
        shape((dp // 2, rows, units), BF),
        shape((dp // 2, per, width), BF),
        shape((dp // 2, per, width), BF),
        shape((sp, chunk, width), BF),
        shape((sp, chunk, width), BF),
        shape((8, width), F32),
        shape((8, width), F32),
        shape((8, wide), F32),
    ]
    scratch = [
        pltpu.VMEM((tokens, width), BF),
        pltpu.VMEM((tokens, width), BF),
        pltpu.VMEM((width, units), BF),
        pltpu.VMEM((units, width), BF),
        pltpu.VMEM((tokens, width), BF),
        pltpu.VMEM((tokens, units), BF),
        pltpu.VMEM((tokens, units), BF),
        pltpu.VMEM((width, units), BF),
        pltpu.VMEM((units, width), BF),
        pltpu.VMEM((dp, 8, width), BF),
        pltpu.VMEM((1, units), F32),
        pltpu.SemaphoreType.DMA((5, max(dp, sp))),
    ]
    return call(
        functools.partial(mlp_kernel, sp, row_n, own_b, len(ew)),
        [ids, *xs, *cots, *ew, *sw],
        [IN_SMEM] + [ANY] * (2 * sp + 2 * len(ew)),
        outs,
        [ANY, ANY, ANY, ANY] + [IN_VMEM] * 5,
        scratch,
        20 * tokens * width * units,
    )


def on_device(
    inputs,
    cotangent,
    joined_weight,
    joined_bias,
    dense_weight,
    dense_bias,
    expand_weight,
    expand_bias,
    shrink_weight,
    shrink_bias,
    attn_gain,
    attn_shift,
    mlp_gain,
    mlp_shift,
):
    seqs, local_len, width = inputs.shape
    sp, dp = lax.axis_size("sp"), lax.axis_size("dp")
    me, dp_me = lax.axis_index("sp"), lax.axis_index("dp")
    heads = HEADS // sp
    local = seqs * local_len
    cols = joined_weight.shape[1] // sp
    wide = -(-cols // LANES) * LANES
    row_n = joined_weight.shape[0]
    rows_d = row_n * sp
    ff_n = shrink_weight.shape[0]
    units = ff_n * dp
    sp_order = cube_order(bits_of(sp))
    dp_order, side_order = cube_order(bits_of(dp)), cube_order(side_first(dp))
    nat = jnp.asarray(sp_order, jnp.int32) ^ me
    near = jnp.asarray(dp_order, jnp.int32) ^ dp_me
    side = jnp.asarray(side_order, jnp.int32) ^ dp_me
    ids = jnp.concatenate([near, nat, me[None], side])
    own_b = joined_bias.shape[0]

    small_parts = (
        joined_bias,
        dense_bias,
        expand_bias,
        shrink_bias,
        attn_gain,
        attn_shift,
        mlp_gain,
        mlp_shift,
    )
    shape = jax.ShapeDtypeStruct
    (both,) = tidy(
        functools.partial(split_weights, sp, dp),
        [expand_weight, joined_weight, *small_parts],
        [shape((sp, 2 * row_n + 8, units), BF)],
    )
    both = lax.all_to_all(both, "sp", split_axis=0, concat_axis=0, tiled=True)
    dense_part = transposed(dense_weight, False)
    expand_pack, joined_part = tidy(
        functools.partial(pack_weights, wide),
        [both],
        [shape((rows_d + 8, units), BF), shape((rows_d, wide), BF)],
    )

    xs = token_blocks(inputs.reshape(local, width), "sp")
    cots = token_blocks(cotangent.reshape(local, width), "sp")
    shrink_w = pieces(shrink_weight, "dp", bits_of(dp))
    expand_w = pieces(expand_pack, "dp", bits_of(dp))
    joined_w = halves(joined_part, "dp", bits_of(dp))
    dense_w = jnp.concatenate(halves(dense_part, "dp", bits_of(dp)), axis=0)
    dense_w = flip_bits(turn_bits(dense_w), "dp").reshape(heads * HD, width)
    pos = (nat[:, None] * local_len + jnp.arange(local_len, dtype=jnp.int32)).reshape(-1)
    lane = jnp.arange(LANES, dtype=jnp.int32) % (ROT // 2)
    freq = 1.0 / 10000.0 ** ((2 * lane).astype(F32) / ROT)
    angles = pos.astype(F32)[:, None] * freq[None, :]
    e_keep, e_send, s_keep, s_send, *parts = feed_forward(
        ids,
        xs,
        cots,
        expand_w,
        shrink_w,
        row_n,
        own_b,
        wide,
    )
    a_keep, a_send, keep, send = attention(
        ids,
        xs,
        cots,
        joined_w,
        dense_w,
        (jnp.cos(angles), jnp.sin(angles)),
        parts,
        seqs,
        heads,
    )

    keep, got = cube_scatter(keep, send, "sp", bits_of(sp))
    output, input_grad = tidy(
        finish_tokens,
        [
            inputs.reshape(local, width),
            cotangent.reshape(local, width),
            keep,
            got,
            parts[3],
        ],
        [shape((local, width), BF), shape((local, width), F32)],
    )
    output, input_grad = output.reshape(inputs.shape), input_grad.reshape(inputs.shape)

    keep, got = cube_scatter(s_keep, s_send, "dp", bits_of(dp))
    shrink_g = keep + got.astype(F32)
    keep, got = cube_scatter(e_keep, e_send, "dp", side_first(dp))
    expands = (keep, got)
    keep, got = cube_scatter(a_keep, a_send, "dp", bits_of(dp))
    last, dense_g = tidy(
        functools.partial(split_grads, sp, cols),
        [keep, got, *expands],
        [shape((sp, 2 * row_n + 8, width), BF), shape((row_n, width), BF)],
    )
    last = lax.all_to_all(last, "sp", split_axis=0, concat_axis=0, tiled=True)
    dense_g = transposed(dense_g, True)
    linear = dp_me * sp + me
    holder = linear * own_b // cols
    starts = [linear * row_n, linear * own_b - holder * cols, dp_me * ff_n]
    at = [holder] + [(width - start) % width for start in starts] + [me]
    joined_g, expand_g, *vectors = tidy(
        functools.partial(join_grads, sp, dp, cols),
        [jnp.stack(at).astype(jnp.int32), last],
        [shape(joined_weight.shape, F32), shape(expand_weight.shape, F32)]
        + [shape((n,), F32) for n in [row_n] * 5 + [own_b, ff_n, row_n]],
    )
    gain_ag, shift_ag, gain_bg, shift_bg, dense_bg, joined_bg, expand_bg, shrink_bg = vectors
    return (
        output,
        input_grad,
        joined_g,
        joined_bg,
        dense_g.astype(F32),
        dense_bg,
        expand_g,
        expand_bg,
        shrink_g,
        shrink_bg,
        gain_ag,
        shift_ag,
        gain_bg,
        shift_bg,
    )


def solution(mesh):
    token = P("dp", "sp", None)
    matrix = P(("dp", "sp"), None)
    vector = P(("dp", "sp"))
    params = (matrix, vector) * 4 + (vector,) * 4
    return jax.shard_map(
        on_device,
        mesh=mesh,
        in_specs=(token, token) + params,
        out_specs=(token, token) + params,
        check_vma=False,
    )
```
